512 devices in a mesh: row: 16 (over x, y), col: 32 (over z, core).
Axes of the slice: x: 4, y: 4, z: 16, core: 2. Of those that a mesh axis runs over, the one named last changes fastest.
Arguments:
- object_field: float32 [2, 2048, 4096], P(None, 'row', 'col'), may hold values from -5 to 5
- probe_modes: float32 [2, 2, 128, 128], replicated, may hold values from -5 to 5
- amplitudes: float32 [16, 32, 2, 128, 128], P('row', 'col'), may hold values from 0.5 to 4
- positions: int32 [16, 32, 2, 2], P('row', 'col'), may hold values from 0 to 127
- counts: int32 [16, 32], P('row', 'col'), may hold values from 1 to 2, as said below
Outputs:
- object_out: float32 [2, 2048, 4096], P(None, 'row', 'col')
- probe_out: float32 [2, 2, 128, 128], replicated
The draws below stay inside these ranges and needn't reach their ends.
Inputs may be any that keep to these rules, and one draw needn't show every extreme that they name: `counts`: slots at or beyond a tile's count hold no frame; in every draw some tile has all 2 slots live.
All inputs are finite; a program needn't handle non-finite values.
Results may differ from the reference program's by a relative error of at most 0.0001.
Values sent between devices are 32-bit elements; how exact they have to be, the bound alone decides.
A program may use at most 64 MiB of HBM per device.

```python
import math
import jax
import jax.numpy as jnp
from jax import lax

W = 128
MODES = 2
TILE = 128
FMAX = 2
INNER = 1
OUTER = 1
TILES_R = 16
TILES_C = 32
NR = 2048
NC = 4096


def draw_counts(key, part):
    keys = jax.random.split(jax.random.fold_in(key, 17), 4)
    base_counts = jax.random.randint(keys[0], (TILES_R, TILES_C), 1, min(3, FMAX) + 1)
    heavy = jax.random.randint(keys[1], (TILES_R, TILES_C), 0, 8) == 0
    result = jnp.where(heavy, FMAX, base_counts)
    pick_row = jax.random.randint(keys[2], (), 0, TILES_R)
    pick_col = jax.random.randint(keys[3], (), 0, TILES_C)
    result = result.at[pick_row, pick_col].set(FMAX)
    return result.astype(jnp.int32)


def with_ends(drawn, own_key, smallest, top_value):
    place = [jax.random.randint(jax.random.fold_in(own_key, axis), (), 0, length) for axis, length in enumerate(drawn.shape)]
    longest = drawn.shape.index(max(drawn.shape))
    neighbour = place[:longest] + [(place[longest] + 1) % drawn.shape[longest]] + place[longest + 1:]
    return drawn.at[tuple(place)].set(smallest).at[tuple(neighbour)].set(top_value)


def shard_levels(key, shape, cuts, least, top_value):
    level = 1.0
    for position, parts in cuts:
        heights = jax.random.uniform(jax.random.fold_in(jax.random.fold_in(key, 6), position), (parts,), jnp.float32, least / len(cuts), top_value / len(cuts))
        level = level * jnp.repeat(jnp.exp(heights), shape[position] // parts).reshape((-1,) + (1,) * (len(shape) - 1 - position))
    return level


def normal_values(key, dims, width, most, shards=(), held_as=jnp.bfloat16):
    drawn = width * jax.random.normal(key, dims, jnp.float32)
    if shards:
        drawn = drawn * shard_levels(key, dims, shards, -0.22, 0.18)
    return jnp.clip(drawn, -most, most).astype(held_as)


def setup_inputs(seed: int = 0) -> dict:
    arg_keys = jax.random.split(jax.random.key(seed), 6)
    return {
        "object_field": normal_values(arg_keys[0], (2, NR, NC), 1.0, 5.0, ((1, 16), (2, 32)), jnp.float32),
        "probe_modes": normal_values(arg_keys[1], (MODES, 2, W, W), 1.0, 5.0, (), jnp.float32),
        "amplitudes": jnp.clip(jnp.exp(math.log(4.0) - 2.0794415 * jax.random.uniform(arg_keys[2], (TILES_R, TILES_C, FMAX, W, W), jnp.float32) ** shard_levels(arg_keys[2], (TILES_R, TILES_C, FMAX, W, W), ((0, 16), (1, 32)), -0.2, 0.2)), 0.5, 4.0),
        "positions": with_ends(jax.random.randint(arg_keys[3], (TILES_R, TILES_C, FMAX, 2), 0, TILE), jax.random.fold_in(arg_keys[3], 1), 0, TILE - 1).astype(jnp.int32),
        "counts": draw_counts(jax.random.fold_in(arg_keys[5], 71), 0),
    }


damping = 1.0

def frame_terms(block_cut, probe_re, probe_im, amplitude):
    o_re = block_cut[0]
    o_im = block_cut[1]
    psi_re = probe_re * o_re - probe_im * o_im
    psi_im = probe_re * o_im + probe_im * o_re
    exit_wave = psi_re + 1j * psi_im
    far_field = jnp.fft.fft2(exit_wave, norm='ortho')
    intensity = lax.optimization_barrier(jnp.sum(jnp.real(far_field) ** 2 + jnp.imag(far_field) ** 2, axis=0))
    modulus = amplitude / jnp.sqrt(intensity + 1.0)
    back_wave = jnp.fft.ifft2(far_field * modulus, norm='ortho')
    return (jnp.real(back_wave) - psi_re, jnp.imag(back_wave) - psi_im)

def one_pass(object_field, probe_modes, amp_flat, top_rows, left_cols, live_flags):
    rim_len = W // 2
    padded = jnp.pad(object_field, ((0, 0), (rim_len, rim_len), (rim_len, rim_len)))
    probe_re = probe_modes[:, 0]
    probe_im = probe_modes[:, 1]
    probe_power = lax.optimization_barrier(jnp.sum(probe_re * probe_re + probe_im * probe_im, axis=0))
    anchor = jnp.int32(0)

    def visit_frame(state_now, frame_item):
        gradient, probe_num, probe_den = state_now
        amplitude, top_row, left_col, live_flag = frame_item
        block_cut = lax.dynamic_slice(padded, (anchor, top_row, left_col), (2, W, W))
        d_re, d_im = frame_terms(block_cut, probe_re, probe_im, amplitude)
        d_re = d_re * live_flag
        d_im = d_im * live_flag
        n_re = lax.optimization_barrier(jnp.sum(probe_re * d_re + probe_im * d_im, axis=0))
        n_im = lax.optimization_barrier(jnp.sum(probe_re * d_im - probe_im * d_re, axis=0))
        deposit = jnp.stack([n_re, n_im, live_flag * probe_power])
        existing = lax.dynamic_slice(gradient, (anchor, top_row, left_col), (3, W, W))
        gradient = lax.dynamic_update_slice(gradient, existing + deposit, (anchor, top_row, left_col))
        o_re = block_cut[0]
        o_im = block_cut[1]
        q_re = o_re * d_re + o_im * d_im
        q_im = o_re * d_im - o_im * d_re
        probe_num = probe_num + jnp.stack([q_re, q_im], axis=1)
        probe_den = probe_den + live_flag * (o_re * o_re + o_im * o_im)
        return ((gradient, probe_num, probe_den), None)
    start_state = (jnp.zeros((3,) + padded.shape[1:], object_field.dtype), jnp.zeros(probe_modes.shape, object_field.dtype), jnp.zeros((W, W), object_field.dtype))
    (gradient, probe_num, probe_den), _ = lax.scan(visit_frame, start_state, (amp_flat, top_rows, left_cols, live_flags))
    summed = gradient[:, rim_len:rim_len + object_field.shape[1], rim_len:rim_len + object_field.shape[2]]
    updated = object_field + summed[0:2] / (summed[2:3] + damping)
    return (updated, probe_num, probe_den)

def reference(object_field, probe_modes, amplitudes, positions, counts):
    amp_flat = amplitudes.reshape(-1, W, W)
    row_base = jnp.arange(TILES_R, dtype=jnp.int32)[:, None, None] * TILE
    col_base = jnp.arange(TILES_C, dtype=jnp.int32)[None, :, None] * TILE
    top_rows = (row_base + positions[..., 0]).reshape(-1).astype(jnp.int32)
    left_cols = (col_base + positions[..., 1]).reshape(-1).astype(jnp.int32)
    slot_ids = jnp.arange(FMAX, dtype=jnp.int32)[None, None, :]
    live_flags = (slot_ids < counts[:, :, None]).astype(object_field.dtype).reshape(-1)
    current = object_field
    probe_now = probe_modes
    for outer_step in range(OUTER):
        for inner_step in range(INNER):
            current, probe_num, probe_den = one_pass(current, probe_now, amp_flat, top_rows, left_cols, live_flags)
        probe_now = probe_now + probe_num / (probe_den + damping)
    return (current, probe_now)
```

```python
import functools

import jax
import jax.numpy as jnp
import numpy as np
from jax import lax
from jax.experimental import pallas as pl
from jax.experimental.pallas import tpu as pltpu
from jax.sharding import PartitionSpec as P

damping = 1.0
MESH = pl.DeviceIdType.MESH
f32 = jnp.float32
bf16 = jnp.bfloat16
VMEM = pl.BlockSpec(memory_space=pltpu.VMEM)
SMEM = pl.BlockSpec(memory_space=pltpu.SMEM)


def dft_parts(size):
    index = np.arange(size)
    angles = (index[:, None] * index[None, :] % size) * (2.0 * np.pi / size)
    cosine, sine = np.cos(angles) / np.sqrt(size), np.sin(angles) / np.sqrt(size)
    right = np.block([[cosine, -sine], [sine, cosine]])
    parts = []
    for table in (right, right.T):
        head = table.astype(bf16)
        parts += [head, (table - head.astype(np.float64)).astype(bf16)]
    return [jnp.asarray(part) for part in parts]


def split(value):
    head = value.astype(bf16)
    return head, (value - head.astype(f32)).astype(bf16)


def dot3(left, right):
    (lh, ll), (rh, rl) = left, right
    dot = functools.partial(jnp.dot, preferred_element_type=f32)
    return dot(lh, rh) + (dot(lh, rl) + dot(ll, rh))


def lanes(shape):
    return lax.broadcasted_iota(jnp.int32, shape, len(shape) - 1)


def halo_kernel(rows, cols, obj, mid, lft, rgt, pack_l, pack_r, send, recv):
    row, col = lax.axis_index("row"), lax.axis_index("col")
    up, dn = lax.rem(row + rows - 1, rows), lax.rem(row + 1, rows)
    le, ri = lax.rem(col + cols - 1, cols), lax.rem(col + 1, cols)
    barrier = pltpu.get_barrier_semaphore()
    around = [(up, col), (dn, col), (row, le), (row, ri), (up, le), (up, ri), (dn, le), (dn, ri)]
    for peer in around:
        pl.semaphore_signal(barrier, inc=1, device_id=peer, device_id_type=MESH)
    size = obj.shape[1]
    half = size // 2
    low = lanes((size, size)) < half
    re, im = obj[0], obj[1]
    pack_l[...] = jnp.where(low, re, pltpu.roll(im, half, 1))
    pack_r[...] = jnp.where(low, pltpu.roll(re, half, 1), im)
    pl.semaphore_wait(barrier, 8)
    first, last = pl.ds(0, half), pl.ds(half, half)
    head, body, tail = pl.ds(0, half), pl.ds(half, size), pl.ds(half + size, half)
    plan = [
        (obj.at[:, last], mid.at[:, head], (dn, col)),
        (obj.at[:, first], mid.at[:, tail], (up, col)),
        (pack_r.at[last], lft.at[head], (dn, ri)),
        (pack_l.at[last], rgt.at[head], (dn, le)),
        (pack_r.at[first], lft.at[tail], (up, ri)),
        (pack_l.at[first], rgt.at[tail], (up, le)),
        (pack_r, lft.at[body], (row, ri)),
        (pack_l, rgt.at[body], (row, le)),
    ]
    copies = []
    for i, (src, dst, peer) in enumerate(plan):
        copy = pltpu.make_async_remote_copy(
            src_ref=src,
            dst_ref=dst,
            send_sem=send.at[i],
            recv_sem=recv.at[i],
            device_id=peer,
            device_id_type=MESH,
        )
        copy.start()
        copies.append(copy)
    mid[:, body] = obj[...]
    for copy in copies:
        copy.wait()


def fetch_halo(obj, rows, cols):
    size = obj.shape[1]
    return pl.pallas_call(
        functools.partial(halo_kernel, rows, cols),
        out_shape=(
            jax.ShapeDtypeStruct((2, 2 * size, size), f32),
            jax.ShapeDtypeStruct((2 * size, size), f32),
            jax.ShapeDtypeStruct((2 * size, size), f32),
        ),
        in_specs=[VMEM],
        out_specs=(VMEM, VMEM, VMEM),
        scratch_shapes=[
            pltpu.VMEM((size, size), f32),
            pltpu.VMEM((size, size), f32),
            pltpu.SemaphoreType.DMA((8,)),
            pltpu.SemaphoreType.DMA((8,)),
        ],
        compiler_params=pltpu.CompilerParams(collective_id=0, has_side_effects=True),
        name="halo",
    )(obj)


def pass_kernel(
    rows,
    cols,
    pos,
    cnt,
    mid,
    lft,
    rgt,
    probe,
    amp,
    mh,
    ml,
    th,
    tl,
    obj_out,
    probe_out,
    pad,
    dep_c,
    dep_s,
    side_l,
    side_r,
    got_l,
    got_r,
    fold,
    got_u,
    got_d,
    terms,
    pair_in,
    pair_sum,
    plane_in,
    plane_sum,
    depth_in,
    fresh,
    gathered,
    s1,
    r1,
    s2,
    r2,
    s3,
    r3,
    s4,
    r4,
    s5,
    r5,
    s6,
    r6,
):
    row, col = lax.axis_index("row"), lax.axis_index("col")
    up, dn = lax.rem(row + rows - 1, rows), lax.rem(row + 1, rows)
    le, ri = lax.rem(col + cols - 1, cols), lax.rem(col + 1, cols)
    deep = cols // 2
    core, z = lax.rem(col, 2), lax.div(col, 2)
    mate = col + 1 - 2 * core
    other = lax.rem(col + 2 * core - 1 + cols, cols)

    barrier = pltpu.get_barrier_semaphore()
    peers = [(row, mate), (row, other)]
    for k in range(1, rows):
        peers += [(lax.rem(row + k, rows), col), (lax.rem(row + k, rows), mate)]
    for k in range(1, deep):
        peers.append((row, 2 * lax.rem(z + k, deep) + core))
    for peer in peers:
        pl.semaphore_signal(barrier, inc=1, device_id=peer, device_id_type=MESH)

    slots, size = amp.shape[0], amp.shape[1]
    modes = probe.shape[0]
    half = size // 2
    lane = lanes((size, size))
    low = lane < half

    wide = lanes((2 * size, size))
    low2 = wide < half
    line = lax.broadcasted_iota(jnp.int32, (2 * size, size), 0)
    first_row = jnp.where(row > 0, 0, half)
    end_row = jnp.where(row < rows - 1, 2 * size, half + size)
    inside = (line >= first_row) & (line < end_row)
    in_l = inside & ((wide >= half) | (wide < jnp.where(col > 0, half, 0)))
    in_r = inside & ((wide < half) | (wide >= jnp.where(col < cols - 1, half, size)))
    lft_v, rgt_v = lft[...], rgt[...]
    for ch in range(2):
        turned = pltpu.roll(mid[ch], half, 1)
        from_l = lft_v if ch == 0 else pltpu.roll(lft_v, half, 1)
        from_r = pltpu.roll(rgt_v, half, 1) if ch == 0 else rgt_v
        pad[ch, 0] = jnp.where(in_l, jnp.where(low2, from_l, turned), 0.0)
        pad[ch, 1] = jnp.where(in_r, jnp.where(low2, turned, from_r), 0.0)

    right = (mh[...], ml[...])
    left = (th[...], tl[...])
    patches, waves = [], []
    for s in range(slots):
        r, c = pos[s, 0], pos[s, 1]
        shift = lax.rem(size - c, size)
        patch = []
        for ch in range(2):
            near = pltpu.roll(pad[ch, 0, pl.ds(r, size)], shift, 1)
            far = pltpu.roll(pad[ch, 1, pl.ds(r, size)], shift, 1)
            patch.append(jnp.where(lane < size - c, near, far))
        patches.append(patch)
        for k in range(modes):
            p_re, p_im = probe[k, 0], probe[k, 1]
            waves.append(
                (p_re * patch[0] - p_im * patch[1], p_re * patch[1] + p_im * patch[0])
            )

    def columns(stacked):
        cut = [stacked[i * size : (i + 1) * size] for i in range(len(waves))]
        return jnp.concatenate(
            [jnp.concatenate([c[:, 0:size], c[:, size : 2 * size]], axis=0) for c in cut], axis=1
        )

    def rows_of(placed):
        cut = [placed[:, i * size : (i + 1) * size] for i in range(len(waves))]
        return jnp.concatenate(
            [jnp.concatenate([c[0:size], c[size : 2 * size]], axis=1) for c in cut], axis=0
        )

    stacked = jnp.concatenate([jnp.concatenate(w, axis=1) for w in waves], axis=0)
    far_field = dot3(left, split(columns(dot3(split(stacked), right))))
    shaped = []
    for s in range(slots):
        block = far_field[:, s * modes * size : (s + 1) * modes * size]
        power = block * block
        power = power[0:size] + power[size : 2 * size]
        intensity = sum(power[:, k * size : (k + 1) * size] for k in range(modes))
        modulus = amp[s] * lax.rsqrt(intensity + 1.0)
        both = jnp.concatenate([modulus, modulus], axis=0)
        shaped += [block[:, k * size : (k + 1) * size] * both for k in range(modes)]
    back = dot3(split(rows_of(dot3(right, split(jnp.concatenate(shaped, axis=1))))), left)

    zero = jnp.zeros((size, size), f32)
    probe_power = zero
    for k in range(modes):
        probe_power += probe[k, 0] * probe[k, 0] + probe[k, 1] * probe[k, 1]
    totals = [[zero, zero] for _ in range(modes)]
    density = zero
    for s in range(slots):
        live = jnp.where(s < cnt[0, 0], 1.0, 0.0)
        o_re, o_im = patches[s]
        n_re, n_im = zero, zero
        for k in range(modes):
            i = s * modes + k
            b = back[i * size : (i + 1) * size]
            d_re = (b[:, 0:size] - waves[i][0]) * live
            d_im = (b[:, size : 2 * size] - waves[i][1]) * live
            p_re, p_im = probe[k, 0], probe[k, 1]
            n_re += p_re * d_re + p_im * d_im
            n_im += p_re * d_im - p_im * d_re
            totals[k][0] += o_re * d_re + o_im * d_im
            totals[k][1] += o_re * d_im - o_im * d_re
        density += live * (o_re * o_re + o_im * o_im)
        c = pos[s, 1]
        shift = lax.rem(c + half, size)
        center = (lane < c + half) & (lane >= c - half)
        for ch, value in enumerate((n_re, n_im, live * probe_power)):
            turned = pltpu.roll(value, shift, 1)
            dep_c[s, ch, size : 2 * size] = jnp.where(center, turned, 0.0)
            dep_s[s, ch, size : 2 * size] = jnp.where(center, 0.0, turned)
            for edge in (0, 2 * size):
                dep_c[s, ch, edge : edge + size] = zero
                dep_s[s, ch, edge : edge + size] = zero

    share = size // rows
    for k in range(modes):
        for i in range(rows):
            cut = slice(i * share, (i + 1) * share)
            terms[k, i, 0] = totals[k][0][cut]
            terms[k, i, 1] = totals[k][1][cut]
            terms[k, i, 2] = density[cut]

    def placed(store, ch):
        return sum(store[s, ch, pl.ds(size - pos[s, 0], 2 * size)] for s in range(slots))

    aside = [placed(dep_s, ch) for ch in range(3)]
    turned = pltpu.roll(aside[1], half, 1)
    side_l[0 : 2 * size] = jnp.where(low2, turned, aside[0])
    side_r[0 : 2 * size] = jnp.where(low2, aside[0], turned)
    w_head, w_tail = aside[2][0:size], pltpu.roll(aside[2][size : 2 * size], half, 1)
    side_l[2 * size : 3 * size] = jnp.where(low, w_tail, w_head)
    side_r[2 * size : 3 * size] = jnp.where(low, w_head, w_tail)

    pl.semaphore_wait(barrier, len(peers))

    def send(src, dst, ssem, rsem, peer):
        copy = pltpu.make_async_remote_copy(
            src_ref=src,
            dst_ref=dst,
            send_sem=ssem,
            recv_sem=rsem,
            device_id=peer,
            device_id_type=MESH,
        )
        copy.start()
        return copy

    pending = []
    to_mate = send(terms.at[1 - core], pair_in, s1.at[0], r1.at[0], (row, mate))
    to_left = send(side_l, got_r, s5.at[0], r5.at[0], (row, le))
    to_right = send(side_r, got_l, s5.at[1], r5.at[1], (row, ri))
    to_mate.wait()
    pair_sum[...] = terms[core] + pair_in[...]

    plane = []
    for k in range(1, rows):
        peer = lax.rem(row + k, rows)
        plane.append(
            send(pair_sum.at[peer], plane_in.at[row], s2.at[k], r2.at[k], (peer, col))
        )
    plane_in[row] = pair_sum[row]
    for copy in plane:
        copy.wait()
    reduced = plane_in[0]
    for i in range(1, rows):
        reduced += plane_in[i]
    plane_sum[...] = reduced

    depth = []
    for k in range(1, deep):
        peer = 2 * lax.rem(z + k, deep) + core
        depth.append(send(plane_sum, depth_in.at[z], s3.at[k], r3.at[k], (row, peer)))
    depth_in[z] = plane_sum[...]

    to_left.wait()
    to_right.wait()
    high = jnp.where(col < cols - 1, 1.0, 0.0)
    base = jnp.where(col > 0, 1.0, 0.0)
    by_l, by_r = got_l[...] * base, got_r[...] * high
    low3 = lanes((3 * size, size)) < half
    plain = jnp.where(low3, by_l, by_r)
    crossed = pltpu.roll(jnp.where(low3, by_r, by_l), half, 1)
    fold[0] = placed(dep_c, 0) + plain[0 : 2 * size]
    fold[1] = placed(dep_c, 1) + crossed[0 : 2 * size]
    weights = jnp.concatenate([plain[2 * size : 3 * size], crossed[2 * size : 3 * size]], axis=0)
    fold[2] = placed(dep_c, 2) + weights
    to_up = send(fold.at[:, 0:half], got_d, s6.at[0], r6.at[0], (up, col))
    to_dn = send(
        fold.at[:, half + size : 2 * size], got_u, s6.at[1], r6.at[1], (dn, col)
    )

    for copy in depth:
        copy.wait()
    total = depth_in[0]
    for i in range(1, deep):
        total += depth_in[i]
    for ch in range(2):
        cut = pl.ds(pl.multiple_of(row * share, share), share)
        fresh[ch] = probe[core, ch, cut] + total[ch] / (total[2] + damping)

    spread = [send(fresh, gathered.at[core, row], s4.at[0], r4.at[0], (row, mate))]
    for k in range(1, rows):
        peer = lax.rem(row + k, rows)
        for j, target in enumerate((col, mate)):
            i = 2 * k + j
            spread.append(
                send(fresh, gathered.at[core, row], s4.at[i], r4.at[i], (peer, target))
            )
    gathered[core, row] = fresh[...]

    to_up.wait()
    to_dn.wait()
    above = got_u[...] * jnp.where(row > 0, 1.0, 0.0)
    below = got_d[...] * jnp.where(row < rows - 1, 1.0, 0.0)
    summed = fold[:, half : half + size] + jnp.concatenate([above, below], axis=1)
    obj_out[...] = mid[:, half : half + size] + summed[0:2] / (summed[2:3] + damping)

    for copy in spread:
        copy.wait()
    for k in range(modes):
        for i in range(rows):
            for ch in range(2):
                probe_out[k, ch, i * share : (i + 1) * share] = gathered[k, i, ch]


def run_pass(pos, cnt, halo, probe, amp, rows, cols):
    slots, size = amp.shape[0], amp.shape[1]
    modes = probe.shape[0]
    deep, share, half = cols // 2, size // rows, size // 2
    dma = pltpu.SemaphoreType.DMA
    return pl.pallas_call(
        functools.partial(pass_kernel, rows, cols),
        out_shape=(
            jax.ShapeDtypeStruct((2, size, size), f32),
            jax.ShapeDtypeStruct(probe.shape, f32),
        ),
        in_specs=[SMEM, SMEM] + [VMEM] * 9,
        out_specs=(VMEM, VMEM),
        scratch_shapes=[
            pltpu.VMEM((2, 2, 2 * size, size), f32),
            pltpu.VMEM((slots, 3, 3 * size, size), f32),
            pltpu.VMEM((slots, 3, 3 * size, size), f32),
            pltpu.VMEM((3 * size, size), f32),
            pltpu.VMEM((3 * size, size), f32),
            pltpu.VMEM((3 * size, size), f32),
            pltpu.VMEM((3 * size, size), f32),
            pltpu.VMEM((3, 2 * size, size), f32),
            pltpu.VMEM((3, half, size), f32),
            pltpu.VMEM((3, half, size), f32),
            pltpu.VMEM((modes, rows, 3, share, size), f32),
            pltpu.VMEM((rows, 3, share, size), f32),
            pltpu.VMEM((rows, 3, share, size), f32),
            pltpu.VMEM((rows, 3, share, size), f32),
            pltpu.VMEM((3, share, size), f32),
            pltpu.VMEM((deep, 3, share, size), f32),
            pltpu.VMEM((2, share, size), f32),
            pltpu.VMEM((modes, rows, 2, share, size), f32),
            dma((1,)),
            dma((1,)),
            dma((rows,)),
            dma((rows,)),
            dma((deep,)),
            dma((deep,)),
            dma((2 * rows,)),
            dma((2 * rows,)),
            dma((2,)),
            dma((2,)),
            dma((2,)),
            dma((2,)),
        ],
        compiler_params=pltpu.CompilerParams(collective_id=1, has_side_effects=True),
        name="object_pass",
    )(pos, cnt, *halo, probe, amp, *dft_parts(size))


def on_device(rows, cols, object_field, probe_modes, amplitudes, positions, counts):
    halo = fetch_halo(object_field, rows, cols)
    return run_pass(positions[0, 0], counts, halo, probe_modes, amplitudes[0, 0], rows, cols)


def solution(mesh):
    rows, cols = mesh.shape["row"], mesh.shape["col"]
    return jax.shard_map(
        functools.partial(on_device, rows, cols),
        mesh=mesh,
        in_specs=(
            P(None, "row", "col"),
            P(),
            P("row", "col", None, None, None),
            P("row", "col", None, None),
            P("row", "col"),
        ),
        out_specs=(P(None, "row", "col"), P()),
        check_vma=False,
    )
```

```python
import functools
import math

import jax
import jax.numpy as jnp
import numpy as np
from jax import lax
from jax.experimental import pallas as pl
from jax.experimental.pallas import tpu as pltpu
from jax.sharding import PartitionSpec as P

damping = 1.0
MESH = pl.DeviceIdType.MESH
f32 = jnp.float32
bf16 = jnp.bfloat16
VMEM = pl.BlockSpec(memory_space=pltpu.VMEM)
SMEM = pl.BlockSpec(memory_space=pltpu.SMEM)
HBM = pl.BlockSpec(memory_space=pltpu.HBM)


def dft_parts(size):
    index = np.arange(size)
    angles = (index[:, None] * index[None, :] % size) * (2.0 * np.pi / size)
    cosine, sine = np.cos(angles) / np.sqrt(size), np.sin(angles) / np.sqrt(size)
    right = np.block([[cosine, -sine], [sine, cosine]])
    parts = []
    for table in (right, right.T):
        head = table.astype(bf16)
        parts += [head, (table - head.astype(np.float64)).astype(bf16)]
    return jnp.asarray(np.stack(parts))


def split(value):
    head = value.astype(bf16)
    return head, (value - head.astype(f32)).astype(bf16)


def dot3(left, right):
    (lh, ll), (rh, rl) = left, right
    dot = functools.partial(jnp.dot, preferred_element_type=f32)
    return dot(lh, rh) + (dot(lh, rl) + dot(ll, rh))


def lanes(shape):
    return lax.broadcasted_iota(jnp.int32, shape, len(shape) - 1)


def pass_kernel(
    rows,
    cols,
    pos,
    cnt,
    obj_in,
    probe_in,
    amp_in,
    tables_in,
    obj_out,
    gathered,
    obj,
    probe,
    amp,
    tables,
    pack_l,
    pack_r,
    mid,
    lft,
    rgt,
    pad,
    dep_c,
    dep_s,
    side_l,
    side_r,
    got_l,
    got_r,
    fold,
    got_u,
    got_d,
    terms,
    pair_in,
    pair_sum,
    plane_in,
    plane_sum,
    depth_in,
    fresh,
    rel,
    s0,
    r0,
    s1,
    r1,
    s2,
    r2,
    s3,
    r3,
    s4,
    r4,
    s5,
    r5,
    s6,
    r6,
):
    row, col = lax.axis_index("row"), lax.axis_index("col")
    up, dn = lax.rem(row + rows - 1, rows), lax.rem(row + 1, rows)
    le, ri = lax.rem(col + cols - 1, cols), lax.rem(col + 1, cols)
    deep = cols // 2
    core, z = lax.rem(col, 2), lax.div(col, 2)
    mate = col + 1 - 2 * core
    other = lax.rem(col + 2 * core - 1 + cols, cols)
    above_z = 2 * lax.rem(z + 1, deep) + core
    below_z = 2 * lax.rem(z + deep - 1, deep) + core

    side = math.isqrt(rows)
    x, y = lax.div(row, side), lax.rem(row, side)

    def hops(d, n):
        return min(d, n - d)

    offsets = sorted(
        ((dx, dy) for dx in range(side) for dy in range(side) if dx or dy),
        key=lambda o: (-hops(o[0], side) - hops(o[1], side), o),
    )
    plane_peers = [
        (dx * side + dy, lax.rem(x + dx, side) * side + lax.rem(y + dy, side))
        for dx, dy in offsets
    ]
    depth_peers = [
        (k, 2 * lax.rem(z + k, deep) + core)
        for k in sorted(range(1, deep), key=lambda k: (-hops(k, deep), k))
    ]

    barrier = pltpu.get_barrier_semaphore()
    near = [(row, mate), (row, other), (up, other), (dn, other), (row, above_z), (row, below_z)]
    for _, peer in plane_peers:
        near += [(peer, col), (peer, mate)]
    for peer in near:
        pl.semaphore_signal(barrier, inc=1, device_id=peer, device_id_type=MESH)

    def send(src, dst, ssem, rsem, peer):
        copy = pltpu.make_async_remote_copy(
            src_ref=src,
            dst_ref=dst,
            send_sem=ssem,
            recv_sem=rsem,
            device_id=peer,
            device_id_type=MESH,
        )
        copy.start()
        return copy

    fetches = []
    for i, (src, dst) in enumerate(
        ((obj_in, obj), (probe_in, probe), (tables_in, tables), (amp_in, amp))
    ):
        fetch = pltpu.make_async_copy(src, dst, s0.at[8 + i])
        fetch.start()
        fetches.append(fetch)

    slots, size = amp.shape[0], amp.shape[1]
    modes = probe.shape[0]
    half = size // 2
    lane = lanes((size, size))
    low = lane < half

    fetches[0].wait()
    re, im = obj[0], obj[1]
    pack_l[...] = jnp.where(low, re, pltpu.roll(im, half, 1))
    pack_r[...] = jnp.where(low, pltpu.roll(re, half, 1), im)
    pl.semaphore_wait(barrier, len(near))

    left_over = [deep // 2 - 1]

    def announce():
        pl.semaphore_signal(rel.at[0], inc=1, device_id=(row, above_z), device_id_type=MESH)
        pl.semaphore_signal(rel.at[1], inc=1, device_id=(row, below_z), device_id_type=MESH)

    def relay(times):
        for _ in range(min(times, left_over[0])):
            pl.semaphore_wait(rel.at[0], 1)
            pl.semaphore_wait(rel.at[1], 1)
            announce()
            left_over[0] -= 1

    announce()
    first, last = pl.ds(0, half), pl.ds(half, half)
    head, body, tail = pl.ds(0, half), pl.ds(half, size), pl.ds(half + size, half)
    plan = [
        (pack_r.at[last], lft.at[head], (dn, ri)),
        (pack_l.at[last], rgt.at[head], (dn, le)),
        (pack_r.at[first], lft.at[tail], (up, ri)),
        (pack_l.at[first], rgt.at[tail], (up, le)),
        (obj.at[:, last], mid.at[:, head], (dn, col)),
        (obj.at[:, first], mid.at[:, tail], (up, col)),
        (pack_r, lft.at[body], (row, ri)),
        (pack_l, rgt.at[body], (row, le)),
    ]
    copies = [send(src, dst, s0.at[i], r0.at[i], peer) for i, (src, dst, peer) in enumerate(plan)]
    mid[:, body] = obj[...]
    for copy in copies[6:]:
        copy.wait()
    relay(1)
    for copy in copies[:6]:
        copy.wait()
    relay(1)
    for fetch in fetches[1:]:
        fetch.wait()

    wide = lanes((2 * size, size))
    low2 = wide < half
    line = lax.broadcasted_iota(jnp.int32, (2 * size, size), 0)
    first_row = jnp.where(row > 0, 0, half)
    end_row = jnp.where(row < rows - 1, 2 * size, half + size)
    inside = (line >= first_row) & (line < end_row)
    in_l = inside & ((wide >= half) | (wide < jnp.where(col > 0, half, 0)))
    in_r = inside & ((wide < half) | (wide >= jnp.where(col < cols - 1, half, size)))
    lft_v, rgt_v = lft[...], rgt[...]
    for ch in range(2):
        turned = pltpu.roll(mid[ch], half, 1)
        from_l = lft_v if ch == 0 else pltpu.roll(lft_v, half, 1)
        from_r = pltpu.roll(rgt_v, half, 1) if ch == 0 else rgt_v
        pad[ch, 0] = jnp.where(in_l, jnp.where(low2, from_l, turned), 0.0)
        pad[ch, 1] = jnp.where(in_r, jnp.where(low2, turned, from_r), 0.0)

    right = (tables[0], tables[1])
    left = (tables[2], tables[3])
    patches, waves = [], []
    for s in range(slots):
        r, c = pos[s, 0], pos[s, 1]
        shift = lax.rem(size - c, size)
        patch = []
        for ch in range(2):
            near = pltpu.roll(pad[ch, 0, pl.ds(r, size)], shift, 1)
            far = pltpu.roll(pad[ch, 1, pl.ds(r, size)], shift, 1)
            patch.append(jnp.where(lane < size - c, near, far))
        patches.append(patch)
        for k in range(modes):
            p_re, p_im = probe[k, 0], probe[k, 1]
            waves.append(
                (p_re * patch[0] - p_im * patch[1], p_re * patch[1] + p_im * patch[0])
            )

    def columns(stacked):
        cut = [stacked[i * size : (i + 1) * size] for i in range(len(waves))]
        return jnp.concatenate(
            [jnp.concatenate([c[:, 0:size], c[:, size : 2 * size]], axis=0) for c in cut], axis=1
        )

    def rows_of(placed):
        cut = [placed[:, i * size : (i + 1) * size] for i in range(len(waves))]
        return jnp.concatenate(
            [jnp.concatenate([c[0:size], c[size : 2 * size]], axis=1) for c in cut], axis=0
        )

    stacked = jnp.concatenate([jnp.concatenate(w, axis=1) for w in waves], axis=0)
    far_field = dot3(left, split(columns(dot3(split(stacked), right))))
    shaped = []
    for s in range(slots):
        block = far_field[:, s * modes * size : (s + 1) * modes * size]
        power = block * block
        power = power[0:size] + power[size : 2 * size]
        intensity = sum(power[:, k * size : (k + 1) * size] for k in range(modes))
        modulus = amp[s] * lax.rsqrt(intensity + 1.0)
        both = jnp.concatenate([modulus, modulus], axis=0)
        shaped += [block[:, k * size : (k + 1) * size] * both for k in range(modes)]
    back = dot3(split(rows_of(dot3(right, split(jnp.concatenate(shaped, axis=1))))), left)

    zero = jnp.zeros((size, size), f32)
    probe_power = zero
    for k in range(modes):
        probe_power += probe[k, 0] * probe[k, 0] + probe[k, 1] * probe[k, 1]
    totals = [[zero, zero] for _ in range(modes)]
    density = zero
    for s in range(slots):
        live = jnp.where(s < cnt[0, 0], 1.0, 0.0)
        o_re, o_im = patches[s]
        n_re, n_im = zero, zero
        for k in range(modes):
            i = s * modes + k
            b = back[i * size : (i + 1) * size]
            d_re = (b[:, 0:size] - waves[i][0]) * live
            d_im = (b[:, size : 2 * size] - waves[i][1]) * live
            p_re, p_im = probe[k, 0], probe[k, 1]
            n_re += p_re * d_re + p_im * d_im
            n_im += p_re * d_im - p_im * d_re
            totals[k][0] += o_re * d_re + o_im * d_im
            totals[k][1] += o_re * d_im - o_im * d_re
        density += live * (o_re * o_re + o_im * o_im)
        c = pos[s, 1]
        shift = lax.rem(c + half, size)
        center = (lane < c + half) & (lane >= c - half)
        for ch, value in enumerate((n_re, n_im, live * probe_power)):
            turned = pltpu.roll(value, shift, 1)
            dep_c[s, ch, size : 2 * size] = jnp.where(center, turned, 0.0)
            dep_s[s, ch, size : 2 * size] = jnp.where(center, 0.0, turned)
            for edge in (0, 2 * size):
                dep_c[s, ch, edge : edge + size] = zero
                dep_s[s, ch, edge : edge + size] = zero

    share = size // rows
    for k in range(modes):
        for i in range(rows):
            cut = slice(i * share, (i + 1) * share)
            terms[k, i, 0] = totals[k][0][cut]
            terms[k, i, 1] = totals[k][1][cut]
            terms[k, i, 2] = density[cut]

    def placed(store, ch):
        return sum(store[s, ch, pl.ds(size - pos[s, 0], 2 * size)] for s in range(slots))

    aside = [placed(dep_s, ch) for ch in range(3)]
    turned = pltpu.roll(aside[1], half, 1)
    side_l[0 : 2 * size] = jnp.where(low2, turned, aside[0])
    side_r[0 : 2 * size] = jnp.where(low2, aside[0], turned)
    w_head, w_tail = aside[2][0:size], pltpu.roll(aside[2][size : 2 * size], half, 1)
    side_l[2 * size : 3 * size] = jnp.where(low, w_tail, w_head)
    side_r[2 * size : 3 * size] = jnp.where(low, w_head, w_tail)

    to_mate = send(terms.at[1 - core], pair_in, s1.at[0], r1.at[0], (row, mate))
    to_left = send(side_l, got_r, s5.at[0], r5.at[0], (row, le))
    to_right = send(side_r, got_l, s5.at[1], r5.at[1], (row, ri))
    relay(2)
    to_mate.wait()
    pair_sum[...] = terms[core] + pair_in[...]

    plane = [
        send(pair_sum.at[peer], plane_in.at[row], s2.at[k], r2.at[k], (peer, col))
        for k, peer in plane_peers
    ]
    plane_in[row] = pair_sum[row]
    relay(deep)
    for copy in plane:
        copy.wait()
    reduced = plane_in[0]
    for i in range(1, rows):
        reduced += plane_in[i]
    plane_sum[...] = reduced

    pl.semaphore_wait(rel.at[0], 1)
    pl.semaphore_wait(rel.at[1], 1)
    depth = [
        send(plane_sum, depth_in.at[z], s3.at[k], r3.at[k], (row, peer)) for k, peer in depth_peers
    ]
    depth_in[z] = plane_sum[...]

    to_left.wait()
    to_right.wait()
    high = jnp.where(col < cols - 1, 1.0, 0.0)
    base = jnp.where(col > 0, 1.0, 0.0)
    by_l, by_r = got_l[...] * base, got_r[...] * high
    low3 = lanes((3 * size, size)) < half
    plain = jnp.where(low3, by_l, by_r)
    crossed = pltpu.roll(jnp.where(low3, by_r, by_l), half, 1)
    fold[0] = placed(dep_c, 0) + plain[0 : 2 * size]
    fold[1] = placed(dep_c, 1) + crossed[0 : 2 * size]
    weights = jnp.concatenate([plain[2 * size : 3 * size], crossed[2 * size : 3 * size]], axis=0)
    fold[2] = placed(dep_c, 2) + weights
    to_up = send(fold.at[:, 0:half], got_d, s6.at[0], r6.at[0], (up, col))
    to_dn = send(
        fold.at[:, half + size : 2 * size], got_u, s6.at[1], r6.at[1], (dn, col)
    )

    for copy in depth:
        copy.wait()
    total = depth_in[0]
    for i in range(1, deep):
        total += depth_in[i]
    for ch in range(2):
        cut = pl.ds(pl.multiple_of(row * share, share), share)
        fresh[ch] = probe[core, ch, cut] + total[ch] / (total[2] + damping)

    spread = [send(fresh, gathered.at[core, row], s4.at[0], r4.at[0], (row, mate))]
    for k, peer in plane_peers:
        for j, target in enumerate((col, mate)):
            i = 2 * k + j
            spread.append(
                send(fresh, gathered.at[core, row], s4.at[i], r4.at[i], (peer, target))
            )
    gathered[core, row] = fresh[...]

    to_up.wait()
    to_dn.wait()
    above = got_u[...] * jnp.where(row > 0, 1.0, 0.0)
    below = got_d[...] * jnp.where(row < rows - 1, 1.0, 0.0)
    summed = fold[:, half : half + size] + jnp.concatenate([above, below], axis=1)
    obj_out[...] = obj[...] + summed[0:2] / (summed[2:3] + damping)

    for copy in spread:
        copy.wait()


def finish_kernel(new_obj, gathered, obj_out, probe_out):
    obj_out[...] = new_obj[...]
    modes, rows, _, share, _ = gathered.shape
    for k in range(modes):
        for i in range(rows):
            for ch in range(2):
                probe_out[k, ch, i * share : (i + 1) * share] = gathered[k, i, ch]


def run_pass(pos, cnt, obj, probe, amp, rows, cols):
    slots, size = amp.shape[0], amp.shape[1]
    modes = probe.shape[0]
    deep, share, half = cols // 2, size // rows, size // 2
    dma = pltpu.SemaphoreType.DMA
    tables = dft_parts(size)
    new_obj, gathered = pl.pallas_call(
        functools.partial(pass_kernel, rows, cols),
        out_shape=(
            jax.ShapeDtypeStruct((2, size, size), f32),
            jax.ShapeDtypeStruct((modes, rows, 2, share, size), f32),
        ),
        in_specs=[SMEM, SMEM] + [HBM] * 4,
        out_specs=(VMEM, VMEM),
        scratch_shapes=[
            pltpu.VMEM((2, size, size), f32),
            pltpu.VMEM(probe.shape, f32),
            pltpu.VMEM(amp.shape, f32),
            pltpu.VMEM(tables.shape, bf16),
            pltpu.VMEM((size, size), f32),
            pltpu.VMEM((size, size), f32),
            pltpu.VMEM((2, 2 * size, size), f32),
            pltpu.VMEM((2 * size, size), f32),
            pltpu.VMEM((2 * size, size), f32),
            pltpu.VMEM((2, 2, 2 * size, size), f32),
            pltpu.VMEM((slots, 3, 3 * size, size), f32),
            pltpu.VMEM((slots, 3, 3 * size, size), f32),
            pltpu.VMEM((3 * size, size), f32),
            pltpu.VMEM((3 * size, size), f32),
            pltpu.VMEM((3 * size, size), f32),
            pltpu.VMEM((3 * size, size), f32),
            pltpu.VMEM((3, 2 * size, size), f32),
            pltpu.VMEM((3, half, size), f32),
            pltpu.VMEM((3, half, size), f32),
            pltpu.VMEM((modes, rows, 3, share, size), f32),
            pltpu.VMEM((rows, 3, share, size), f32),
            pltpu.VMEM((rows, 3, share, size), f32),
            pltpu.VMEM((rows, 3, share, size), f32),
            pltpu.VMEM((3, share, size), f32),
            pltpu.VMEM((deep, 3, share, size), f32),
            pltpu.VMEM((2, share, size), f32),
            pltpu.SemaphoreType.REGULAR((2,)),
            dma((12,)),
            dma((8,)),
            dma((1,)),
            dma((1,)),
            dma((rows,)),
            dma((rows,)),
            dma((deep,)),
            dma((deep,)),
            dma((2 * rows,)),
            dma((2 * rows,)),
            dma((2,)),
            dma((2,)),
            dma((2,)),
            dma((2,)),
        ],
        compiler_params=pltpu.CompilerParams(
            collective_id=0, has_side_effects=True, vmem_limit_bytes=20 * 2**20
        ),
        name="object_pass",
    )(pos, cnt, *(pltpu.with_memory_space_constraint(a, pltpu.HBM) for a in (obj, probe, amp, tables)))
    return pl.pallas_call(
        finish_kernel,
        out_shape=(
            jax.ShapeDtypeStruct((2, size, size), f32),
            jax.ShapeDtypeStruct(probe.shape, f32),
        ),
        in_specs=[VMEM, VMEM],
        out_specs=(VMEM, VMEM),
        compiler_params=pltpu.CompilerParams(vmem_limit_bytes=4 * 2**20),
        name="finish",
    )(new_obj, gathered)


def on_device(rows, cols, object_field, probe_modes, amplitudes, positions, counts):
    return run_pass(
        positions[0, 0], counts, object_field, probe_modes, amplitudes[0, 0], rows, cols
    )


def solution(mesh):
    rows, cols = mesh.shape["row"], mesh.shape["col"]
    return jax.shard_map(
        functools.partial(on_device, rows, cols),
        mesh=mesh,
        in_specs=(
            P(None, "row", "col"),
            P(),
            P("row", "col", None, None, None),
            P("row", "col", None, None),
            P("row", "col"),
        ),
        out_specs=(P(None, "row", "col"), P()),
        check_vma=False,
    )
```

```python
import functools
import math

import jax
import jax.numpy as jnp
import numpy as np
from jax import lax
from jax.experimental import pallas as pl
from jax.experimental.pallas import tpu as pltpu
from jax.sharding import PartitionSpec as P

damping = 1.0
MESH = pl.DeviceIdType.MESH
f32 = jnp.float32
bf16 = jnp.bfloat16
VMEM = pl.BlockSpec(memory_space=pltpu.VMEM)
SMEM = pl.BlockSpec(memory_space=pltpu.SMEM)
HBM = pl.BlockSpec(memory_space=pltpu.HBM)


def dft_parts(size):
    index = np.arange(size)
    angles = (index[:, None] * index[None, :] % size) * (2.0 * np.pi / size)
    cosine, sine = np.cos(angles) / np.sqrt(size), np.sin(angles) / np.sqrt(size)
    right = np.block([[cosine, -sine], [sine, cosine]])
    parts = []
    for table in (right, right.T):
        head = table.astype(bf16)
        parts += [head, (table - head.astype(np.float64)).astype(bf16)]
    return jnp.asarray(np.stack(parts))


def split(value):
    head = value.astype(bf16)
    return head, (value - head.astype(f32)).astype(bf16)


def dot3(left, right):
    (lh, ll), (rh, rl) = left, right
    dot = functools.partial(jnp.dot, preferred_element_type=f32)
    return dot(lh, rh) + (dot(lh, rl) + dot(ll, rh))


def in_hbm(value):
    return pltpu.with_memory_space_constraint(value, pltpu.HBM)


def lanes(shape):
    return lax.broadcasted_iota(jnp.int32, shape, len(shape) - 1)


def pass_kernel(
    rows,
    cols,
    pos_in,
    cnt,
    obj_in,
    probe_in,
    amp_in,
    tables_in,
    obj_out,
    gathered,
    obj,
    probe,
    amp,
    tables,
    pack_l,
    pack_r,
    mid,
    lft,
    rgt,
    pad,
    dep_c,
    dep_s,
    side_l,
    side_r,
    got_l,
    got_r,
    fold,
    got_u,
    got_d,
    terms,
    pair_in,
    pair_sum,
    plane_in,
    plane_sum,
    depth_in,
    fresh,
    pos,
    rel,
    s0,
    r0,
    s1,
    r1,
    s2,
    r2,
    s3,
    r3,
    s4,
    r4,
    s5,
    r5,
    s6,
    r6,
):
    row, col = lax.axis_index("row"), lax.axis_index("col")
    up, dn = lax.rem(row + rows - 1, rows), lax.rem(row + 1, rows)
    le, ri = lax.rem(col + cols - 1, cols), lax.rem(col + 1, cols)
    deep = cols // 2
    core, z = lax.rem(col, 2), lax.div(col, 2)
    mate = col + 1 - 2 * core
    above_z = 2 * lax.rem(z + 1, deep) + core
    below_z = 2 * lax.rem(z + deep - 1, deep) + core

    twin = col + 2 - 4 * lax.rem(z, 2)
    half_z, odd = lax.div(z, 2), lax.rem(z, 2)
    pairs = deep // 2

    side = math.isqrt(rows)
    x, y = lax.div(row, side), lax.rem(row, side)

    def hops(d, n):
        return min(d, n - d)

    def chip(dx, dy):
        return lax.rem(x + dx, side) * side + lax.rem(y + dy, side)

    offsets = sorted(
        ((dx, dy) for dx in range(side) for dy in range(side)),
        key=lambda o: (-hops(o[0], side) - hops(o[1], side), o),
    )
    plane_peers = [(dx * side + dy, chip(dx, dy)) for dx, dy in offsets]
    depth_peers = [
        (k, 2 * lax.rem(z + 2 * k, deep) + core)
        for k in sorted(range(1, pairs), key=lambda k: (-hops(k, pairs), k))
    ]

    barrier = pltpu.get_barrier_semaphore()
    beside = [
        (chip(1, 0), col),
        (chip(side - 1, 0), col),
        (chip(0, 1), col),
        (chip(0, side - 1), col),
        (row, above_z),
        (row, below_z),
    ]
    near = [(up, col), (dn, col), (row, le), (row, ri), (up, le), (up, ri), (dn, le), (dn, ri)]
    near += beside
    for peer in near:
        pl.semaphore_signal(barrier, inc=1, device_id=peer, device_id_type=MESH)

    def send(src, dst, ssem, rsem, peer):
        copy = pltpu.make_async_remote_copy(
            src_ref=src,
            dst_ref=dst,
            send_sem=ssem,
            recv_sem=rsem,
            device_id=peer,
            device_id_type=MESH,
        )
        copy.start()
        return copy

    fetches = []
    for i, (src, dst) in enumerate(
        (
            (obj_in, obj),
            (pos_in, pos),
            (probe_in, probe),
            (tables_in, tables),
            (amp_in, amp),
        )
    ):
        fetch = pltpu.make_async_copy(src, dst, s0.at[8 + i])
        fetch.start()
        fetches.append(fetch)

    slots, size = amp.shape[0], amp.shape[1]
    modes = probe.shape[0]
    half = size // 2
    lane = lanes((size, size))
    low = lane < half

    fetches[0].wait()
    re, im = obj[0], obj[1]
    pack_l[...] = jnp.where(low, re, pltpu.roll(im, half, 1))
    pack_r[...] = jnp.where(low, pltpu.roll(re, half, 1), im)
    pl.semaphore_wait(barrier, len(near))

    plane_rounds, depth_rounds = 2 * (side // 2), deep // 2 - 1
    rounds = iter(range(1, max(plane_rounds, depth_rounds) + 1))

    def ways(step):
        plane_ways = range(4) if step <= plane_rounds else ()
        return (*plane_ways, *((4, 5) if step <= depth_rounds else ()))

    def announce(step):
        for i in ways(step):
            pl.semaphore_signal(
                rel.at[i], inc=1, device_id=beside[i], device_id_type=MESH
            )

    def relay(upto):
        for step in rounds:
            for i in ways(step):
                pl.semaphore_wait(rel.at[i], 1)
            announce(step + 1)
            if step >= upto:
                return

    announce(1)
    first, last = pl.ds(0, half), pl.ds(half, half)
    head, body, tail = pl.ds(0, half), pl.ds(half, size), pl.ds(half + size, half)
    plan = [
        (pack_r.at[last], lft.at[head], (dn, ri)),
        (pack_l.at[last], rgt.at[head], (dn, le)),
        (pack_r.at[first], lft.at[tail], (up, ri)),
        (pack_l.at[first], rgt.at[tail], (up, le)),
        (obj.at[:, last], mid.at[:, head], (dn, col)),
        (obj.at[:, first], mid.at[:, tail], (up, col)),
        (pack_r, lft.at[body], (row, ri)),
        (pack_l, rgt.at[body], (row, le)),
    ]
    copies = [send(src, dst, s0.at[i], r0.at[i], peer) for i, (src, dst, peer) in enumerate(plan)]
    mid[:, body] = obj[...]
    for copy in copies[6:]:
        copy.wait()
    relay(1)
    for copy in copies[:6]:
        copy.wait()
    relay(2)
    for fetch in fetches[1:]:
        fetch.wait()

    wide = lanes((2 * size, size))
    low2 = wide < half
    line = lax.broadcasted_iota(jnp.int32, (2 * size, size), 0)
    first_row = jnp.where(row > 0, 0, half)
    end_row = jnp.where(row < rows - 1, 2 * size, half + size)
    inside = (line >= first_row) & (line < end_row)
    in_l = inside & ((wide >= half) | (wide < jnp.where(col > 0, half, 0)))
    in_r = inside & ((wide < half) | (wide >= jnp.where(col < cols - 1, half, size)))
    lft_v, rgt_v = lft[...], rgt[...]
    for ch in range(2):
        turned = pltpu.roll(mid[ch], half, 1)
        from_l = lft_v if ch == 0 else pltpu.roll(lft_v, half, 1)
        from_r = pltpu.roll(rgt_v, half, 1) if ch == 0 else rgt_v
        pad[ch, 0] = jnp.where(in_l, jnp.where(low2, from_l, turned), 0.0)
        pad[ch, 1] = jnp.where(in_r, jnp.where(low2, turned, from_r), 0.0)

    right = (tables[0], tables[1])
    left = (tables[2], tables[3])
    patches, waves = [], []
    for s in range(slots):
        r, c = pos[s, 0], pos[s, 1]
        shift = lax.rem(size - c, size)
        patch = []
        for ch in range(2):
            near = pltpu.roll(pad[ch, 0, pl.ds(r, size)], shift, 1)
            far = pltpu.roll(pad[ch, 1, pl.ds(r, size)], shift, 1)
            patch.append(jnp.where(lane < size - c, near, far))
        patches.append(patch)
        for k in range(modes):
            p_re, p_im = probe[k, 0], probe[k, 1]
            waves.append(
                (p_re * patch[0] - p_im * patch[1], p_re * patch[1] + p_im * patch[0])
            )

    def columns(stacked):
        cut = [stacked[i * size : (i + 1) * size] for i in range(len(waves))]
        return jnp.concatenate(
            [jnp.concatenate([c[:, 0:size], c[:, size : 2 * size]], axis=0) for c in cut], axis=1
        )

    def rows_of(placed):
        cut = [placed[:, i * size : (i + 1) * size] for i in range(len(waves))]
        return jnp.concatenate(
            [jnp.concatenate([c[0:size], c[size : 2 * size]], axis=1) for c in cut], axis=0
        )

    stacked = jnp.concatenate([jnp.concatenate(w, axis=1) for w in waves], axis=0)
    far_field = dot3(left, split(columns(dot3(split(stacked), right))))
    shaped = []
    for s in range(slots):
        block = far_field[:, s * modes * size : (s + 1) * modes * size]
        power = block * block
        power = power[0:size] + power[size : 2 * size]
        intensity = sum(power[:, k * size : (k + 1) * size] for k in range(modes))
        modulus = amp[s] * lax.rsqrt(intensity + 1.0)
        both = jnp.concatenate([modulus, modulus], axis=0)
        shaped += [block[:, k * size : (k + 1) * size] * both for k in range(modes)]
    back = dot3(split(rows_of(dot3(right, split(jnp.concatenate(shaped, axis=1))))), left)

    zero = jnp.zeros((size, size), f32)
    probe_power = zero
    for k in range(modes):
        probe_power += probe[k, 0] * probe[k, 0] + probe[k, 1] * probe[k, 1]
    totals = [[zero, zero] for _ in range(modes)]
    density = zero
    for s in range(slots):
        live = jnp.where(s < cnt[0, 0], 1.0, 0.0)
        o_re, o_im = patches[s]
        n_re, n_im = zero, zero
        for k in range(modes):
            i = s * modes + k
            b = back[i * size : (i + 1) * size]
            d_re = (b[:, 0:size] - waves[i][0]) * live
            d_im = (b[:, size : 2 * size] - waves[i][1]) * live
            p_re, p_im = probe[k, 0], probe[k, 1]
            n_re += p_re * d_re + p_im * d_im
            n_im += p_re * d_im - p_im * d_re
            totals[k][0] += o_re * d_re + o_im * d_im
            totals[k][1] += o_re * d_im - o_im * d_re
        density += live * (o_re * o_re + o_im * o_im)
        c = pos[s, 1]
        shift = lax.rem(c + half, size)
        center = (lane < c + half) & (lane >= c - half)
        for ch, value in enumerate((n_re, n_im, live * probe_power)):
            turned = pltpu.roll(value, shift, 1)
            dep_c[s, ch, size : 2 * size] = jnp.where(center, turned, 0.0)
            dep_s[s, ch, size : 2 * size] = jnp.where(center, 0.0, turned)
            for edge in (0, 2 * size):
                dep_c[s, ch, edge : edge + size] = zero
                dep_s[s, ch, edge : edge + size] = zero

    share = size // rows
    part = share // 2
    for k in range(modes):
        for i in range(rows):
            for j in range(2):
                cut = slice(i * share + j * part, i * share + (j + 1) * part)
                terms[k, i, j, 0] = totals[k][0][cut]
                terms[k, i, j, 1] = totals[k][1][cut]
                terms[k, i, j, 2] = density[cut]

    def placed(store, ch):
        return sum(store[s, ch, pl.ds(size - pos[s, 0], 2 * size)] for s in range(slots))

    aside = [placed(dep_s, ch) for ch in range(3)]
    turned = pltpu.roll(aside[1], half, 1)
    side_l[0 : 2 * size] = jnp.where(low2, turned, aside[0])
    side_r[0 : 2 * size] = jnp.where(low2, aside[0], turned)
    w_head, w_tail = aside[2][0:size], pltpu.roll(aside[2][size : 2 * size], half, 1)
    side_l[2 * size : 3 * size] = jnp.where(low, w_tail, w_head)
    side_r[2 * size : 3 * size] = jnp.where(low, w_head, w_tail)

    to_mate = [
        (send(terms.at[1 - core, peer], pair_in.at[peer], s1.at[k], r1.at[k], (row, mate)), k, peer)
        for k, peer in plane_peers
    ]
    relay(plane_rounds)

    plane = []
    for copy, k, peer in to_mate:
        copy.wait()
        pair_sum[peer] = terms[core, peer] + pair_in[peer]
        plane.append(
            send(
                pair_sum.at[peer, 1 - odd],
                plane_in.at[odd, row],
                s2.at[rows + k],
                r2.at[rows + k],
                (peer, twin),
            )
        )
        if k:
            plane.append(
                send(pair_sum.at[peer, odd], plane_in.at[odd, row], s2.at[k], r2.at[k], (peer, col))
            )
    to_left = send(side_l, got_r, s5.at[0], r5.at[0], (row, le))
    to_right = send(side_r, got_l, s5.at[1], r5.at[1], (row, ri))
    plane_in[odd, row] = pair_sum[row, odd]
    relay(deep)
    for copy in plane:
        copy.wait()
    reduced = plane_in[0, 0]
    for i in range(1, 2 * rows):
        reduced += plane_in[i // rows, i % rows]
    plane_sum[...] = reduced

    depth = [
        send(plane_sum, depth_in.at[half_z], s3.at[k], r3.at[k], (row, peer))
        for k, peer in depth_peers
    ]
    depth_in[half_z] = plane_sum[...]

    to_left.wait()
    to_right.wait()
    high = jnp.where(col < cols - 1, 1.0, 0.0)
    base = jnp.where(col > 0, 1.0, 0.0)
    by_l, by_r = got_l[...] * base, got_r[...] * high
    low3 = lanes((3 * size, size)) < half
    plain = jnp.where(low3, by_l, by_r)
    crossed = pltpu.roll(jnp.where(low3, by_r, by_l), half, 1)
    fold[0] = placed(dep_c, 0) + plain[0 : 2 * size]
    fold[1] = placed(dep_c, 1) + crossed[0 : 2 * size]
    weights = jnp.concatenate([plain[2 * size : 3 * size], crossed[2 * size : 3 * size]], axis=0)
    fold[2] = placed(dep_c, 2) + weights
    to_up = send(fold.at[:, 0:half], got_d, s6.at[0], r6.at[0], (up, col))
    to_dn = send(
        fold.at[:, half + size : 2 * size], got_u, s6.at[1], r6.at[1], (dn, col)
    )

    for copy in depth:
        copy.wait()
    total = depth_in[0]
    for i in range(1, pairs):
        total += depth_in[i]
    for ch in range(2):
        cut = pl.ds(row * share + odd * part, part)
        fresh[ch] = probe[core, ch, cut] + total[ch] / (total[2] + damping)

    spread = []
    for k, peer in plane_peers:
        across = 2 * (half_z * 2 + 1 - odd) + 1 - core
        for j, target in enumerate((across, twin, mate, col)):
            if k or j < 3:
                i = 4 * k + j
                spread.append(
                    send(fresh, gathered.at[core, row, odd], s4.at[i], r4.at[i], (peer, target))
                )
    gathered[core, row, odd] = fresh[...]

    to_up.wait()
    to_dn.wait()
    above = got_u[...] * jnp.where(row > 0, 1.0, 0.0)
    below = got_d[...] * jnp.where(row < rows - 1, 1.0, 0.0)
    summed = fold[:, half : half + size] + jnp.concatenate([above, below], axis=1)
    obj_out[...] = obj[...] + summed[0:2] / (summed[2:3] + damping)

    for copy in spread:
        copy.wait()


def finish_kernel(new_obj, gathered, obj_out, probe_out):
    obj_out[...] = new_obj[...]
    modes, rows, _, _, part, _ = gathered.shape
    for k in range(modes):
        for i in range(2 * rows):
            for ch in range(2):
                probe_out[k, ch, i * part : (i + 1) * part] = gathered[k, i // 2, i % 2, ch]


def run_pass(pos, cnt, obj, probe, amp, rows, cols):
    slots, size = amp.shape[0], amp.shape[1]
    modes = probe.shape[0]
    deep, part, half = cols // 2, size // rows // 2, size // 2
    dma = pltpu.SemaphoreType.DMA
    tables = dft_parts(size)
    new_obj, gathered = pl.pallas_call(
        functools.partial(pass_kernel, rows, cols),
        out_shape=(
            jax.ShapeDtypeStruct((2, size, size), f32),
            jax.ShapeDtypeStruct((modes, rows, 2, 2, part, size), f32),
        ),
        in_specs=[HBM, SMEM] + [HBM] * 4,
        out_specs=(VMEM, VMEM),
        scratch_shapes=[
            pltpu.VMEM((2, size, size), f32),
            pltpu.VMEM(probe.shape, f32),
            pltpu.VMEM(amp.shape, f32),
            pltpu.VMEM(tables.shape, bf16),
            pltpu.VMEM((size, size), f32),
            pltpu.VMEM((size, size), f32),
            pltpu.VMEM((2, 2 * size, size), f32),
            pltpu.VMEM((2 * size, size), f32),
            pltpu.VMEM((2 * size, size), f32),
            pltpu.VMEM((2, 2, 2 * size, size), f32),
            pltpu.VMEM((slots, 3, 3 * size, size), f32),
            pltpu.VMEM((slots, 3, 3 * size, size), f32),
            pltpu.VMEM((3 * size, size), f32),
            pltpu.VMEM((3 * size, size), f32),
            pltpu.VMEM((3 * size, size), f32),
            pltpu.VMEM((3 * size, size), f32),
            pltpu.VMEM((3, 2 * size, size), f32),
            pltpu.VMEM((3, half, size), f32),
            pltpu.VMEM((3, half, size), f32),
            pltpu.VMEM((modes, rows, 2, 3, part, size), f32),
            pltpu.VMEM((rows, 2, 3, part, size), f32),
            pltpu.VMEM((rows, 2, 3, part, size), f32),
            pltpu.VMEM((2, rows, 3, part, size), f32),
            pltpu.VMEM((3, part, size), f32),
            pltpu.VMEM((deep // 2, 3, part, size), f32),
            pltpu.VMEM((2, part, size), f32),
            pltpu.SMEM(pos.shape, jnp.int32),
            pltpu.SemaphoreType.REGULAR((6,)),
            dma((13,)),
            dma((8,)),
            dma((rows,)),
            dma((rows,)),
            dma((2 * rows,)),
            dma((2 * rows,)),
            dma((deep // 2,)),
            dma((deep // 2,)),
            dma((4 * rows,)),
            dma((4 * rows,)),
            dma((2,)),
            dma((2,)),
            dma((2,)),
            dma((2,)),
        ],
        compiler_params=pltpu.CompilerParams(
            collective_id=0, has_side_effects=True, vmem_limit_bytes=20 * 2**20
        ),
        name="object_pass",
    )(in_hbm(pos), cnt, in_hbm(obj), in_hbm(probe), in_hbm(amp), in_hbm(tables))
    return pl.pallas_call(
        finish_kernel,
        out_shape=(
            jax.ShapeDtypeStruct((2, size, size), f32),
            jax.ShapeDtypeStruct(probe.shape, f32),
        ),
        in_specs=[VMEM, VMEM],
        out_specs=(VMEM, VMEM),
        compiler_params=pltpu.CompilerParams(vmem_limit_bytes=4 * 2**20),
        name="finish",
    )(new_obj, gathered)


def on_device(rows, cols, object_field, probe_modes, amplitudes, positions, counts):
    return run_pass(
        positions[0, 0], counts, object_field, probe_modes, amplitudes[0, 0], rows, cols
    )


def solution(mesh):
    rows, cols = mesh.shape["row"], mesh.shape["col"]
    return jax.shard_map(
        functools.partial(on_device, rows, cols),
        mesh=mesh,
        in_specs=(
            P(None, "row", "col"),
            P(),
            P("row", "col", None, None, None),
            P("row", "col", None, None),
            P("row", "col"),
        ),
        out_specs=(P(None, "row", "col"), P()),
        check_vma=False,
    )
```

```python
import functools
import math

import jax
import jax.numpy as jnp
import numpy as np
from jax import lax
from jax.experimental import pallas as pl
from jax.experimental.pallas import tpu as pltpu
from jax.sharding import PartitionSpec as P

damping = 1.0
MESH = pl.DeviceIdType.MESH
f32 = jnp.float32
bf16 = jnp.bfloat16
VMEM = pl.BlockSpec(memory_space=pltpu.VMEM)
SMEM = pl.BlockSpec(memory_space=pltpu.SMEM)
HBM = pl.BlockSpec(memory_space=pltpu.HBM)


def dft_parts(size):
    index = np.arange(size)
    angles = (index[:, None] * index[None, :] % size) * (2.0 * np.pi / size)
    cosine, sine = np.cos(angles) / np.sqrt(size), np.sin(angles) / np.sqrt(size)
    right = np.block([[cosine, -sine], [sine, cosine]])
    parts = []
    for table in (right, right.T):
        head = table.astype(bf16)
        parts += [head, (table - head.astype(np.float64)).astype(bf16)]
    return jnp.asarray(np.stack(parts))


def split(value):
    head = value.astype(bf16)
    return head, (value - head.astype(f32)).astype(bf16)


def dot3(left, right):
    (lh, ll), (rh, rl) = left, right
    dot = functools.partial(jnp.dot, preferred_element_type=f32)
    both = dot(jnp.concatenate([lh, ll], axis=0), rh)
    rows = lh.shape[0]
    return both[0:rows] + (dot(lh, rl) + both[rows : 2 * rows])


def in_hbm(value):
    return pltpu.with_memory_space_constraint(value, pltpu.HBM)


def lanes(shape):
    return lax.broadcasted_iota(jnp.int32, shape, len(shape) - 1)


def pass_kernel(
    rows,
    cols,
    pos_in,
    cnt,
    obj_in,
    probe_in,
    amp_in,
    tables_in,
    obj_out,
    gathered,
    obj,
    probe,
    amp,
    tables,
    pack_l,
    pack_r,
    mid,
    lft,
    rgt,
    pad,
    dep_c,
    dep_s,
    side_l,
    side_r,
    got_l,
    got_r,
    fold,
    got_u,
    got_d,
    terms,
    pair_in,
    pair_sum,
    plane_in,
    plane_sum,
    depth_in,
    fresh,
    pos,
    rel,
    s0,
    r0,
    s1,
    r1,
    s2,
    r2,
    s3,
    r3,
    s4,
    r4,
    s5,
    r5,
    s6,
    r6,
):
    row, col = lax.axis_index("row"), lax.axis_index("col")
    up, dn = lax.rem(row + rows - 1, rows), lax.rem(row + 1, rows)
    le, ri = lax.rem(col + cols - 1, cols), lax.rem(col + 1, cols)
    deep = cols // 2
    core, z = lax.rem(col, 2), lax.div(col, 2)
    mate = col + 1 - 2 * core
    twin = col + 2 - 4 * lax.rem(z, 2)
    half_z, odd = lax.div(z, 2), lax.rem(z, 2)
    pairs = deep // 2

    side = math.isqrt(rows)
    x, y = lax.div(row, side), lax.rem(row, side)

    def hops(d, n):
        return min(d, n - d)

    def chip(dx, dy):
        return lax.rem(x + dx, side) * side + lax.rem(y + dy, side)

    offsets = sorted(
        ((dx, dy) for dx in range(side) for dy in range(side)),
        key=lambda o: (-hops(o[0], side) - hops(o[1], side), o),
    )
    plane_peers = [(dx * side + dy, chip(dx, dy)) for dx, dy in offsets]
    depth_peers = [
        (k, 2 * lax.rem(z + 2 * k, deep) + core)
        for k in sorted(range(1, pairs), key=lambda k: (-hops(k, pairs), k))
    ]

    barrier = pltpu.get_barrier_semaphore()
    reach, stride = side // 2, -(-(deep // 2) // 3)

    def level(d):
        return 2 * lax.rem(z + deep + d, deep) + core

    near = [(up, col), (dn, col), (row, le), (row, ri), (up, le), (up, ri), (dn, le), (dn, ri)]
    near += [
        (chip(dx, dy), col)
        for dx, dy in offsets
        if 0 < hops(dx, side) + hops(dy, side) <= reach
    ]
    near += [(row, level(d * sign)) for d in range(1, stride + 1) for sign in (1, -1)]
    ends = [(row, level(stride)), (row, level(-stride))]
    told = ([(chip(reach, 0), col), (chip(0, reach), col)] + ends, [(row, twin)] + ends)
    for peer in near:
        pl.semaphore_signal(barrier, inc=1, device_id=peer, device_id_type=MESH)

    def link(src, dst, ssem, rsem, peer):
        return pltpu.make_async_remote_copy(
            src_ref=src,
            dst_ref=dst,
            send_sem=ssem,
            recv_sem=rsem,
            device_id=peer,
            device_id_type=MESH,
        )

    def send(*ends):
        copy = link(*ends)
        copy.start()
        return copy

    fetches = []
    for i, (src, dst) in enumerate(
        (
            (obj_in, obj),
            (pos_in, pos),
            (probe_in, probe),
            (tables_in, tables),
            (amp_in, amp),
        )
    ):
        fetch = pltpu.make_async_copy(src, dst, s0.at[8 + i])
        fetch.start()
        fetches.append(fetch)

    slots, size = amp.shape[0], amp.shape[1]
    modes = probe.shape[0]
    half = size // 2
    lane = lanes((size, size))
    low = lane < half

    fetches[0].wait()
    re, im = obj[0], obj[1]
    pack_l[...] = jnp.where(low, re, pltpu.roll(im, half, 1))
    pack_r[...] = jnp.where(low, pltpu.roll(re, half, 1), im)
    pl.semaphore_wait(barrier, len(near))

    def tell(step):
        for i, peer in enumerate(told[step]):
            pl.semaphore_signal(rel.at[step, i], inc=1, device_id=peer, device_id_type=MESH)

    def hear(step):
        for i in range(len(told[step])):
            pl.semaphore_wait(rel.at[step, i], 1)

    tell(0)
    first, last = pl.ds(0, half), pl.ds(half, half)
    head, body, tail = pl.ds(0, half), pl.ds(half, size), pl.ds(half + size, half)
    plan = [
        (pack_r.at[last], lft.at[head], (dn, ri)),
        (pack_l.at[last], rgt.at[head], (dn, le)),
        (pack_r.at[first], lft.at[tail], (up, ri)),
        (pack_l.at[first], rgt.at[tail], (up, le)),
        (obj.at[:, last], mid.at[:, head], (dn, col)),
        (obj.at[:, first], mid.at[:, tail], (up, col)),
        (pack_r, lft.at[body], (row, ri)),
        (pack_l, rgt.at[body], (row, le)),
    ]
    copies = [send(src, dst, s0.at[i], r0.at[i], peer) for i, (src, dst, peer) in enumerate(plan)]
    mid[:, body] = obj[...]
    border = jnp.zeros((slots, 3, size, size), f32)
    for store in (dep_c, dep_s):
        store[:, :, 0:size] = border
        store[:, :, 2 * size : 3 * size] = border
    for copy in copies[6:]:
        copy.wait()
    hear(0)
    tell(1)
    for copy in copies[:6]:
        copy.wait()
    for fetch in fetches[1:]:
        fetch.wait()

    wide = lanes((2 * size, size))
    low2 = wide < half
    line = lax.broadcasted_iota(jnp.int32, (2 * size, size), 0)
    first_row = jnp.where(row > 0, 0, half)
    end_row = jnp.where(row < rows - 1, 2 * size, half + size)
    inside = (line >= first_row) & (line < end_row)
    in_l = inside & ((wide >= half) | (wide < jnp.where(col > 0, half, 0)))
    in_r = inside & ((wide < half) | (wide >= jnp.where(col < cols - 1, half, size)))
    lft_v, rgt_v = lft[...], rgt[...]
    for ch in range(2):
        turned = pltpu.roll(mid[ch], half, 1)
        from_l = lft_v if ch == 0 else pltpu.roll(lft_v, half, 1)
        from_r = pltpu.roll(rgt_v, half, 1) if ch == 0 else rgt_v
        pad[ch, 0] = jnp.where(in_l, jnp.where(low2, from_l, turned), 0.0)
        pad[ch, 1] = jnp.where(in_r, jnp.where(low2, turned, from_r), 0.0)

    right = (tables[0], tables[1])
    left = (tables[2], tables[3])
    patches, waves = [], []
    for s in range(slots):
        r, c = pos[s, 0], pos[s, 1]
        shift = lax.rem(size - c, size)
        patch = []
        for ch in range(2):
            near = pltpu.roll(pad[ch, 0, pl.ds(r, size)], shift, 1)
            far = pltpu.roll(pad[ch, 1, pl.ds(r, size)], shift, 1)
            patch.append(jnp.where(lane < size - c, near, far))
        patches.append(patch)
        for k in range(modes):
            p_re, p_im = probe[k, 0], probe[k, 1]
            waves.append(
                (p_re * patch[0] - p_im * patch[1], p_re * patch[1] + p_im * patch[0])
            )

    def columns(stacked):
        cut = [stacked[i * size : (i + 1) * size] for i in range(len(waves))]
        return jnp.concatenate(
            [jnp.concatenate([c[:, 0:size], c[:, size : 2 * size]], axis=0) for c in cut], axis=1
        )

    def rows_of(placed):
        cut = [placed[:, i * size : (i + 1) * size] for i in range(len(waves))]
        return jnp.concatenate(
            [jnp.concatenate([c[0:size], c[size : 2 * size]], axis=1) for c in cut], axis=0
        )

    stacked = jnp.concatenate([jnp.concatenate(w, axis=1) for w in waves], axis=0)
    far_field = dot3(left, split(columns(dot3(split(stacked), right))))
    shaped = []
    for s in range(slots):
        block = far_field[:, s * modes * size : (s + 1) * modes * size]
        power = block * block
        power = power[0:size] + power[size : 2 * size]
        intensity = sum(power[:, k * size : (k + 1) * size] for k in range(modes))
        modulus = amp[s] * lax.rsqrt(intensity + 1.0)
        both = jnp.concatenate([modulus, modulus], axis=0)
        shaped += [block[:, k * size : (k + 1) * size] * both for k in range(modes)]
    back = dot3(split(rows_of(dot3(right, split(jnp.concatenate(shaped, axis=1))))), left)

    zero = jnp.zeros((size, size), f32)
    totals = [[zero, zero] for _ in range(modes)]
    density = zero
    changes = []
    for s in range(slots):
        live = jnp.where(s < cnt[0, 0], 1.0, 0.0)
        o_re, o_im = patches[s]
        for k in range(modes):
            i = s * modes + k
            b = back[i * size : (i + 1) * size]
            d_re = (b[:, 0:size] - waves[i][0]) * live
            d_im = (b[:, size : 2 * size] - waves[i][1]) * live
            changes.append((d_re, d_im))
            totals[k][0] += o_re * d_re + o_im * d_im
            totals[k][1] += o_re * d_im - o_im * d_re
        density += live * (o_re * o_re + o_im * o_im)

    share = size // rows
    part = share // 2
    for k in range(modes):
        for i in range(rows):
            for j in range(2):
                cut = slice(i * share + j * part, i * share + (j + 1) * part)
                terms[k, i, j, 0] = totals[k][0][cut]
                terms[k, i, j, 1] = totals[k][1][cut]
                terms[k, i, j, 2] = density[cut]

    to_mate = [
        (send(terms.at[1 - core, peer], pair_in.at[peer], s1.at[k], r1.at[k], (row, mate)), k, peer)
        for k, peer in plane_peers
    ]

    probe_power = zero
    for k in range(modes):
        probe_power += probe[k, 0] * probe[k, 0] + probe[k, 1] * probe[k, 1]
    for s in range(slots):
        live = jnp.where(s < cnt[0, 0], 1.0, 0.0)
        n_re, n_im = zero, zero
        for k in range(modes):
            d_re, d_im = changes[s * modes + k]
            p_re, p_im = probe[k, 0], probe[k, 1]
            n_re += p_re * d_re + p_im * d_im
            n_im += p_re * d_im - p_im * d_re
        c = pos[s, 1]
        shift = lax.rem(c + half, size)
        center = (lane < c + half) & (lane >= c - half)
        for ch, value in enumerate((n_re, n_im, live * probe_power)):
            turned = pltpu.roll(value, shift, 1)
            dep_c[s, ch, size : 2 * size] = jnp.where(center, turned, 0.0)
            dep_s[s, ch, size : 2 * size] = jnp.where(center, 0.0, turned)

    def placed(store, ch):
        return sum(store[s, ch, pl.ds(size - pos[s, 0], 2 * size)] for s in range(slots))

    aside = [placed(dep_s, ch) for ch in range(3)]
    turned = pltpu.roll(aside[1], half, 1)
    side_l[0 : 2 * size] = jnp.where(low2, turned, aside[0])
    side_r[0 : 2 * size] = jnp.where(low2, aside[0], turned)
    w_head, w_tail = aside[2][0:size], pltpu.roll(aside[2][size : 2 * size], half, 1)
    side_l[2 * size : 3 * size] = jnp.where(low, w_tail, w_head)
    side_r[2 * size : 3 * size] = jnp.where(low, w_head, w_tail)

    hear(1)

    plane = []
    for copy, k, peer in to_mate:
        copy.wait()
        pair_sum[peer] = terms[core, peer] + pair_in[peer]
        plane.append(
            send(
                pair_sum.at[peer, 1 - odd],
                plane_in.at[odd, row],
                s2.at[rows + k],
                r2.at[rows + k],
                (peer, twin),
            )
        )
        if k:
            plane.append(
                send(pair_sum.at[peer, odd], plane_in.at[odd, row], s2.at[k], r2.at[k], (peer, col))
            )
    plane_in[odd, row] = pair_sum[row, odd]

    to_left = send(side_l, got_r, s5.at[0], r5.at[0], (row, le))
    to_right = send(side_r, got_l, s5.at[1], r5.at[1], (row, ri))
    for copy in plane:
        copy.wait()
    reduced = plane_in[0, 0]
    for i in range(1, 2 * rows):
        reduced += plane_in[i // rows, i % rows]
    plane_sum[...] = reduced

    depth = [
        send(plane_sum, depth_in.at[half_z], s3.at[k], r3.at[k], (row, peer))
        for k, peer in depth_peers
    ]
    depth_in[half_z] = plane_sum[...]

    to_left.wait()
    to_right.wait()
    high = jnp.where(col < cols - 1, 1.0, 0.0)
    base = jnp.where(col > 0, 1.0, 0.0)
    by_l, by_r = got_l[...] * base, got_r[...] * high
    low3 = lanes((3 * size, size)) < half
    plain = jnp.where(low3, by_l, by_r)
    crossed = pltpu.roll(jnp.where(low3, by_r, by_l), half, 1)
    fold[0] = placed(dep_c, 0) + plain[0 : 2 * size]
    fold[1] = placed(dep_c, 1) + crossed[0 : 2 * size]
    weights = jnp.concatenate([plain[2 * size : 3 * size], crossed[2 * size : 3 * size]], axis=0)
    fold[2] = placed(dep_c, 2) + weights
    to_up = send(fold.at[:, 0:half], got_d, s6.at[0], r6.at[0], (up, col))
    to_dn = send(
        fold.at[:, half + size : 2 * size], got_u, s6.at[1], r6.at[1], (dn, col)
    )

    for copy in depth:
        copy.wait()
    total = depth_in[0]
    for i in range(1, pairs):
        total += depth_in[i]
    for ch in range(2):
        cut = pl.ds(row * share + odd * part, part)
        fresh[ch] = probe[core, ch, cut] + total[ch] / (total[2] + damping)

    spread = []
    for k, peer in plane_peers:
        across = 2 * (half_z * 2 + 1 - odd) + 1 - core
        for j, target in enumerate((across, twin, mate, col)):
            if k or j < 3:
                i = 4 * k + j
                spread.append(
                    send(fresh, gathered.at[core, row, odd], s4.at[i], r4.at[i], (peer, target))
                )
    gathered[core, row, odd] = fresh[...]

    to_up.wait()
    to_dn.wait()
    above = got_u[...] * jnp.where(row > 0, 1.0, 0.0)
    below = got_d[...] * jnp.where(row < rows - 1, 1.0, 0.0)
    summed = fold[:, half : half + size] + jnp.concatenate([above, below], axis=1)
    obj_out[...] = obj[...] + summed[0:2] / (summed[2:3] + damping)

    for copy in spread:
        copy.wait()


def finish_kernel(new_obj, gathered, obj_out, probe_out):
    obj_out[...] = new_obj[...]
    modes, rows, _, _, part, _ = gathered.shape
    for k in range(modes):
        for i in range(2 * rows):
            for ch in range(2):
                probe_out[k, ch, i * part : (i + 1) * part] = gathered[k, i // 2, i % 2, ch]


def run_pass(pos, cnt, obj, probe, amp, rows, cols):
    slots, size = amp.shape[0], amp.shape[1]
    modes = probe.shape[0]
    deep, part, half = cols // 2, size // rows // 2, size // 2
    dma = pltpu.SemaphoreType.DMA
    tables = dft_parts(size)
    new_obj, gathered = pl.pallas_call(
        functools.partial(pass_kernel, rows, cols),
        out_shape=(
            jax.ShapeDtypeStruct((2, size, size), f32),
            jax.ShapeDtypeStruct((modes, rows, 2, 2, part, size), f32),
        ),
        in_specs=[HBM, SMEM] + [HBM] * 4,
        out_specs=(VMEM, VMEM),
        scratch_shapes=[
            pltpu.VMEM((2, size, size), f32),
            pltpu.VMEM(probe.shape, f32),
            pltpu.VMEM(amp.shape, f32),
            pltpu.VMEM(tables.shape, bf16),
            pltpu.VMEM((size, size), f32),
            pltpu.VMEM((size, size), f32),
            pltpu.VMEM((2, 2 * size, size), f32),
            pltpu.VMEM((2 * size, size), f32),
            pltpu.VMEM((2 * size, size), f32),
            pltpu.VMEM((2, 2, 2 * size, size), f32),
            pltpu.VMEM((slots, 3, 3 * size, size), f32),
            pltpu.VMEM((slots, 3, 3 * size, size), f32),
            pltpu.VMEM((3 * size, size), f32),
            pltpu.VMEM((3 * size, size), f32),
            pltpu.VMEM((3 * size, size), f32),
            pltpu.VMEM((3 * size, size), f32),
            pltpu.VMEM((3, 2 * size, size), f32),
            pltpu.VMEM((3, half, size), f32),
            pltpu.VMEM((3, half, size), f32),
            pltpu.VMEM((modes, rows, 2, 3, part, size), f32),
            pltpu.VMEM((rows, 2, 3, part, size), f32),
            pltpu.VMEM((rows, 2, 3, part, size), f32),
            pltpu.VMEM((2, rows, 3, part, size), f32),
            pltpu.VMEM((3, part, size), f32),
            pltpu.VMEM((deep // 2, 3, part, size), f32),
            pltpu.VMEM((2, part, size), f32),
            pltpu.SMEM(pos.shape, jnp.int32),
            pltpu.SemaphoreType.REGULAR((2, 4)),
            dma((13,)),
            dma((8,)),
            dma((rows,)),
            dma((rows,)),
            dma((2 * rows,)),
            dma((2 * rows,)),
            dma((deep // 2,)),
            dma((deep // 2,)),
            dma((4 * rows,)),
            dma((4 * rows,)),
            dma((2,)),
            dma((2,)),
            dma((2,)),
            dma((2,)),
        ],
        compiler_params=pltpu.CompilerParams(
            collective_id=0, has_side_effects=True, vmem_limit_bytes=20 * 2**20
        ),
        name="object_pass",
    )(in_hbm(pos), cnt, in_hbm(obj), in_hbm(probe), in_hbm(amp), in_hbm(tables))
    return pl.pallas_call(
        finish_kernel,
        out_shape=(
            jax.ShapeDtypeStruct((2, size, size), f32),
            jax.ShapeDtypeStruct(probe.shape, f32),
        ),
        in_specs=[VMEM, VMEM],
        out_specs=(VMEM, VMEM),
        compiler_params=pltpu.CompilerParams(vmem_limit_bytes=4 * 2**20),
        name="finish",
    )(new_obj, gathered)


def on_device(rows, cols, object_field, probe_modes, amplitudes, positions, counts):
    return run_pass(
        positions[0, 0], counts, object_field, probe_modes, amplitudes[0, 0], rows, cols
    )


def solution(mesh):
    rows, cols = mesh.shape["row"], mesh.shape["col"]
    return jax.shard_map(
        functools.partial(on_device, rows, cols),
        mesh=mesh,
        in_specs=(
            P(None, "row", "col"),
            P(),
            P("row", "col", None, None, None),
            P("row", "col", None, None),
            P("row", "col"),
        ),
        out_specs=(P(None, "row", "col"), P()),
        check_vma=False,
    )
```

```python
import functools
import math

import jax
import jax.numpy as jnp
import numpy as np
from jax import lax
from jax.experimental import pallas as pl
from jax.experimental.pallas import tpu as pltpu
from jax.sharding import PartitionSpec as P

damping = 1.0
MESH = pl.DeviceIdType.MESH
f32 = jnp.float32
bf16 = jnp.bfloat16
VMEM = pl.BlockSpec(memory_space=pltpu.VMEM)
SMEM = pl.BlockSpec(memory_space=pltpu.SMEM)
HBM = pl.BlockSpec(memory_space=pltpu.HBM)


def dft_parts(size):
    index = np.arange(size)
    angles = (index[:, None] * index[None, :] % size) * (2.0 * np.pi / size)
    cosine, sine = np.cos(angles) / np.sqrt(size), np.sin(angles) / np.sqrt(size)
    right = np.block([[cosine, -sine], [sine, cosine]])
    parts = []
    for table in (right, right.T):
        head = table.astype(bf16)
        parts += [head, (table - head.astype(np.float64)).astype(bf16)]
    return jnp.asarray(np.stack(parts))


def split(value):
    head = value.astype(bf16)
    return head, (value - head.astype(f32)).astype(bf16)


def dot3(left, right):
    (lh, ll), (rh, rl) = left, right
    dot = functools.partial(jnp.dot, preferred_element_type=f32)
    return dot(lh, rh) + (dot(lh, rl) + dot(ll, rh))


def in_hbm(value):
    return pltpu.with_memory_space_constraint(value, pltpu.HBM)


def lanes(shape):
    return lax.broadcasted_iota(jnp.int32, shape, len(shape) - 1)


def pass_kernel(
    rows,
    cols,
    pos_in,
    cnt,
    obj_in,
    probe_in,
    amp_in,
    tables_in,
    obj_out,
    gathered,
    obj,
    probe,
    amp,
    tables,
    pack_l,
    pack_r,
    mid,
    lft,
    rgt,
    pad,
    dep_c,
    dep_s,
    side_l,
    side_r,
    got_l,
    got_r,
    fold,
    got_u,
    got_d,
    terms,
    pair_in,
    pair_sum,
    plane_in,
    plane_sum,
    depth_in,
    fresh,
    pos,
    rel,
    s0,
    r0,
    s1,
    r1,
    s2,
    r2,
    s3,
    r3,
    s4,
    r4,
    s5,
    r5,
    s6,
    r6,
):
    row, col = lax.axis_index("row"), lax.axis_index("col")
    up, dn = lax.rem(row + rows - 1, rows), lax.rem(row + 1, rows)
    le, ri = lax.rem(col + cols - 1, cols), lax.rem(col + 1, cols)
    deep = cols // 2
    core, z = lax.rem(col, 2), lax.div(col, 2)
    mate = col + 1 - 2 * core
    twin = col + 2 - 4 * lax.rem(z, 2)
    half_z, odd = lax.div(z, 2), lax.rem(z, 2)
    pairs = deep // 2

    side = math.isqrt(rows)
    x, y = lax.div(row, side), lax.rem(row, side)

    def hops(d, n):
        return min(d, n - d)

    def chip(dx, dy):
        return lax.rem(x + dx, side) * side + lax.rem(y + dy, side)

    offsets = sorted(
        ((dx, dy) for dx in range(side) for dy in range(side)),
        key=lambda o: (-hops(o[0], side) - hops(o[1], side), o),
    )
    plane_peers = [(dx * side + dy, chip(dx, dy)) for dx, dy in offsets]
    depth_peers = [
        (k, 2 * lax.rem(z + 2 * k, deep) + core)
        for k in sorted(range(1, pairs), key=lambda k: (-hops(k, pairs), k))
    ]

    barrier = pltpu.get_barrier_semaphore()
    reach, stride = side // 2, -(-(deep // 2) // 3)

    def level(d):
        return 2 * lax.rem(z + deep + d, deep) + core

    near = [(up, col), (dn, col), (row, le), (row, ri), (up, le), (up, ri), (dn, le), (dn, ri)]
    near += [
        (chip(dx, dy), col)
        for dx, dy in offsets
        if 0 < hops(dx, side) + hops(dy, side) <= reach
    ]
    near += [(row, level(d * sign)) for d in range(1, stride + 1) for sign in (1, -1)]
    ends = [(row, level(stride)), (row, level(-stride))]
    told = ([(chip(reach, 0), col), (chip(0, reach), col)] + ends, [(row, twin)] + ends)
    for peer in near:
        pl.semaphore_signal(barrier, inc=1, device_id=peer, device_id_type=MESH)

    def link(src, dst, ssem, rsem, peer):
        return pltpu.make_async_remote_copy(
            src_ref=src,
            dst_ref=dst,
            send_sem=ssem,
            recv_sem=rsem,
            device_id=peer,
            device_id_type=MESH,
        )

    def send(*ends):
        copy = link(*ends)
        copy.start()
        return copy

    fetches = []
    for i, (src, dst) in enumerate(
        (
            (obj_in, obj),
            (pos_in, pos),
            (probe_in, probe),
            (tables_in, tables),
            (amp_in, amp),
        )
    ):
        fetch = pltpu.make_async_copy(src, dst, s0.at[8 + i])
        fetch.start()
        fetches.append(fetch)

    slots, size = amp.shape[0], amp.shape[1]
    modes = probe.shape[0]
    half = size // 2
    lane = lanes((size, size))
    low = lane < half

    fetches[0].wait()
    re, im = obj[0], obj[1]
    pack_l[...] = jnp.where(low, re, pltpu.roll(im, half, 1))
    pack_r[...] = jnp.where(low, pltpu.roll(re, half, 1), im)
    pl.semaphore_wait(barrier, len(near))

    def tell(step):
        for i, peer in enumerate(told[step]):
            pl.semaphore_signal(rel.at[step, i], inc=1, device_id=peer, device_id_type=MESH)

    def hear(step):
        for i in range(len(told[step])):
            pl.semaphore_wait(rel.at[step, i], 1)

    tell(0)
    first, last = pl.ds(0, half), pl.ds(half, half)
    head, body, tail = pl.ds(0, half), pl.ds(half, size), pl.ds(half + size, half)
    plan = [
        (pack_r.at[last], lft.at[head], (dn, ri)),
        (pack_l.at[last], rgt.at[head], (dn, le)),
        (pack_r.at[first], lft.at[tail], (up, ri)),
        (pack_l.at[first], rgt.at[tail], (up, le)),
        (obj.at[:, last], mid.at[:, head], (dn, col)),
        (obj.at[:, first], mid.at[:, tail], (up, col)),
        (pack_r, lft.at[body], (row, ri)),
        (pack_l, rgt.at[body], (row, le)),
    ]
    copies = [send(src, dst, s0.at[i], r0.at[i], peer) for i, (src, dst, peer) in enumerate(plan)]
    mid[:, body] = obj[...]
    border = jnp.zeros((slots, 3, size, size), f32)
    for store in (dep_c, dep_s):
        store[:, :, 0:size] = border
        store[:, :, 2 * size : 3 * size] = border
    for copy in copies[6:]:
        copy.wait()
    hear(0)
    tell(1)
    for copy in copies[:6]:
        copy.wait()
    for fetch in fetches[1:]:
        fetch.wait()

    wide = lanes((2 * size, size))
    low2 = wide < half
    line = lax.broadcasted_iota(jnp.int32, (2 * size, size), 0)
    first_row = jnp.where(row > 0, 0, half)
    end_row = jnp.where(row < rows - 1, 2 * size, half + size)
    inside = (line >= first_row) & (line < end_row)
    in_l = inside & ((wide >= half) | (wide < jnp.where(col > 0, half, 0)))
    in_r = inside & ((wide < half) | (wide >= jnp.where(col < cols - 1, half, size)))
    lft_v, rgt_v = lft[...], rgt[...]
    for ch in range(2):
        turned = pltpu.roll(mid[ch], half, 1)
        from_l = lft_v if ch == 0 else pltpu.roll(lft_v, half, 1)
        from_r = pltpu.roll(rgt_v, half, 1) if ch == 0 else rgt_v
        pad[ch, 0] = jnp.where(in_l, jnp.where(low2, from_l, turned), 0.0)
        pad[ch, 1] = jnp.where(in_r, jnp.where(low2, turned, from_r), 0.0)

    right = (tables[0], tables[1])
    left = (tables[2], tables[3])
    patches, waves = [], []
    for s in range(slots):
        r, c = pos[s, 0], pos[s, 1]
        shift = lax.rem(size - c, size)
        patch = []
        for ch in range(2):
            near = pltpu.roll(pad[ch, 0, pl.ds(r, size)], shift, 1)
            far = pltpu.roll(pad[ch, 1, pl.ds(r, size)], shift, 1)
            patch.append(jnp.where(lane < size - c, near, far))
        patches.append(patch)
        for k in range(modes):
            p_re, p_im = probe[k, 0], probe[k, 1]
            waves.append(
                (p_re * patch[0] - p_im * patch[1], p_re * patch[1] + p_im * patch[0])
            )

    def columns(stacked):
        cut = [stacked[i * size : (i + 1) * size] for i in range(len(waves))]
        return jnp.concatenate(
            [jnp.concatenate([c[:, 0:size], c[:, size : 2 * size]], axis=0) for c in cut], axis=1
        )

    def rows_of(placed):
        cut = [placed[:, i * size : (i + 1) * size] for i in range(len(waves))]
        return jnp.concatenate(
            [jnp.concatenate([c[0:size], c[size : 2 * size]], axis=1) for c in cut], axis=0
        )

    stacked = jnp.concatenate([jnp.concatenate(w, axis=1) for w in waves], axis=0)
    far_field = dot3(left, split(columns(dot3(split(stacked), right))))
    shaped = []
    for s in range(slots):
        block = far_field[:, s * modes * size : (s + 1) * modes * size]
        power = block * block
        power = power[0:size] + power[size : 2 * size]
        intensity = sum(power[:, k * size : (k + 1) * size] for k in range(modes))
        modulus = amp[s] * lax.rsqrt(intensity + 1.0)
        both = jnp.concatenate([modulus, modulus], axis=0)
        shaped += [block[:, k * size : (k + 1) * size] * both for k in range(modes)]
    back = dot3(split(rows_of(dot3(right, split(jnp.concatenate(shaped, axis=1))))), left)

    zero = jnp.zeros((size, size), f32)
    totals = [[zero, zero] for _ in range(modes)]
    density = zero
    changes = []
    for s in range(slots):
        live = jnp.where(s < cnt[0, 0], 1.0, 0.0)
        o_re, o_im = patches[s]
        for k in range(modes):
            i = s * modes + k
            b = back[i * size : (i + 1) * size]
            d_re = (b[:, 0:size] - waves[i][0]) * live
            d_im = (b[:, size : 2 * size] - waves[i][1]) * live
            changes.append((d_re, d_im))
            totals[k][0] += o_re * d_re + o_im * d_im
            totals[k][1] += o_re * d_im - o_im * d_re
        density += live * (o_re * o_re + o_im * o_im)

    share = size // rows
    part = share // 2
    for k in range(modes):
        for i in range(rows):
            for j in range(2):
                cut = slice(i * share + j * part, i * share + (j + 1) * part)
                terms[k, i, j, 0] = totals[k][0][cut]
                terms[k, i, j, 1] = totals[k][1][cut]
                terms[k, i, j, 2] = density[cut]

    to_mate = [
        (send(terms.at[1 - core, peer], pair_in.at[peer], s1.at[k], r1.at[k], (row, mate)), k, peer)
        for k, peer in plane_peers
    ]

    probe_power = zero
    for k in range(modes):
        probe_power += probe[k, 0] * probe[k, 0] + probe[k, 1] * probe[k, 1]
    for s in range(slots):
        live = jnp.where(s < cnt[0, 0], 1.0, 0.0)
        n_re, n_im = zero, zero
        for k in range(modes):
            d_re, d_im = changes[s * modes + k]
            p_re, p_im = probe[k, 0], probe[k, 1]
            n_re += p_re * d_re + p_im * d_im
            n_im += p_re * d_im - p_im * d_re
        c = pos[s, 1]
        shift = lax.rem(c + half, size)
        center = (lane < c + half) & (lane >= c - half)
        for ch, value in enumerate((n_re, n_im, live * probe_power)):
            turned = pltpu.roll(value, shift, 1)
            dep_c[s, ch, size : 2 * size] = jnp.where(center, turned, 0.0)
            dep_s[s, ch, size : 2 * size] = jnp.where(center, 0.0, turned)

    def placed(store, ch):
        return sum(store[s, ch, pl.ds(size - pos[s, 0], 2 * size)] for s in range(slots))

    aside = [placed(dep_s, ch) for ch in range(3)]
    turned = pltpu.roll(aside[1], half, 1)
    side_l[0 : 2 * size] = jnp.where(low2, turned, aside[0])
    side_r[0 : 2 * size] = jnp.where(low2, aside[0], turned)
    w_head, w_tail = aside[2][0:size], pltpu.roll(aside[2][size : 2 * size], half, 1)
    side_l[2 * size : 3 * size] = jnp.where(low, w_tail, w_head)
    side_r[2 * size : 3 * size] = jnp.where(low, w_head, w_tail)

    hear(1)

    plane = []
    for copy, k, peer in to_mate:
        copy.wait()
        pair_sum[peer] = terms[core, peer] + pair_in[peer]
        plane.append(
            send(
                pair_sum.at[peer, 1 - odd],
                plane_in.at[odd, row],
                s2.at[rows + k],
                r2.at[rows + k],
                (peer, twin),
            )
        )
        if k:
            plane.append(
                send(pair_sum.at[peer, odd], plane_in.at[odd, row], s2.at[k], r2.at[k], (peer, col))
            )
    plane_in[odd, row] = pair_sum[row, odd]

    to_left = send(side_l, got_r, s5.at[0], r5.at[0], (row, le))
    to_right = send(side_r, got_l, s5.at[1], r5.at[1], (row, ri))
    for copy in plane:
        copy.wait()
    reduced = plane_in[0, 0]
    for i in range(1, 2 * rows):
        reduced += plane_in[i // rows, i % rows]
    plane_sum[...] = reduced

    depth = [
        send(plane_sum, depth_in.at[half_z], s3.at[k], r3.at[k], (row, peer))
        for k, peer in depth_peers
    ]
    depth_in[half_z] = plane_sum[...]

    to_left.wait()
    to_right.wait()
    high = jnp.where(col < cols - 1, 1.0, 0.0)
    base = jnp.where(col > 0, 1.0, 0.0)
    by_l, by_r = got_l[...] * base, got_r[...] * high
    low3 = lanes((3 * size, size)) < half
    plain = jnp.where(low3, by_l, by_r)
    crossed = pltpu.roll(jnp.where(low3, by_r, by_l), half, 1)
    fold[0] = placed(dep_c, 0) + plain[0 : 2 * size]
    fold[1] = placed(dep_c, 1) + crossed[0 : 2 * size]
    weights = jnp.concatenate([plain[2 * size : 3 * size], crossed[2 * size : 3 * size]], axis=0)
    fold[2] = placed(dep_c, 2) + weights
    to_up = send(fold.at[:, 0:half], got_d, s6.at[0], r6.at[0], (up, col))
    to_dn = send(
        fold.at[:, half + size : 2 * size], got_u, s6.at[1], r6.at[1], (dn, col)
    )

    for copy in depth:
        copy.wait()
    total = depth_in[0]
    for i in range(1, pairs):
        total += depth_in[i]
    for ch in range(2):
        cut = pl.ds(row * share + odd * part, part)
        fresh[ch] = probe[core, ch, cut] + total[ch] / (total[2] + damping)

    spread = []
    for k, peer in plane_peers:
        across = 2 * (half_z * 2 + 1 - odd) + 1 - core
        for j, target in enumerate((across, twin, mate, col)):
            if k or j < 3:
                i = 4 * k + j
                spread.append(
                    send(fresh, gathered.at[core, row, odd], s4.at[i], r4.at[i], (peer, target))
                )
    gathered[core, row, odd] = fresh[...]

    to_up.wait()
    to_dn.wait()
    above = got_u[...] * jnp.where(row > 0, 1.0, 0.0)
    below = got_d[...] * jnp.where(row < rows - 1, 1.0, 0.0)
    summed = fold[:, half : half + size] + jnp.concatenate([above, below], axis=1)
    obj_out[...] = obj[...] + summed[0:2] / (summed[2:3] + damping)

    for copy in spread:
        copy.wait()


def finish_kernel(new_obj, gathered, obj_out, probe_out, probe_new, sems):
    keep = pltpu.make_async_copy(new_obj, obj_out, sems.at[0])
    keep.start()
    modes, rows, _, _, part, _ = gathered.shape
    stores = []
    for k in range(modes):
        for i in range(2 * rows):
            for ch in range(2):
                probe_new[k, ch, i * part : (i + 1) * part] = gathered[k, i // 2, i % 2, ch]
        store = pltpu.make_async_copy(probe_new.at[k], probe_out.at[k], sems.at[1 + k])
        store.start()
        stores.append(store)
    keep.wait()
    for store in stores:
        store.wait()


def run_pass(pos, cnt, obj, probe, amp, rows, cols):
    slots, size = amp.shape[0], amp.shape[1]
    modes = probe.shape[0]
    deep, part, half = cols // 2, size // rows // 2, size // 2
    dma = pltpu.SemaphoreType.DMA
    tables = dft_parts(size)
    new_obj, gathered = pl.pallas_call(
        functools.partial(pass_kernel, rows, cols),
        out_shape=(
            jax.ShapeDtypeStruct((2, size, size), f32),
            jax.ShapeDtypeStruct((modes, rows, 2, 2, part, size), f32),
        ),
        in_specs=[HBM, SMEM] + [HBM] * 4,
        out_specs=(VMEM, VMEM),
        scratch_shapes=[
            pltpu.VMEM((2, size, size), f32),
            pltpu.VMEM(probe.shape, f32),
            pltpu.VMEM(amp.shape, f32),
            pltpu.VMEM(tables.shape, bf16),
            pltpu.VMEM((size, size), f32),
            pltpu.VMEM((size, size), f32),
            pltpu.VMEM((2, 2 * size, size), f32),
            pltpu.VMEM((2 * size, size), f32),
            pltpu.VMEM((2 * size, size), f32),
            pltpu.VMEM((2, 2, 2 * size, size), f32),
            pltpu.VMEM((slots, 3, 3 * size, size), f32),
            pltpu.VMEM((slots, 3, 3 * size, size), f32),
            pltpu.VMEM((3 * size, size), f32),
            pltpu.VMEM((3 * size, size), f32),
            pltpu.VMEM((3 * size, size), f32),
            pltpu.VMEM((3 * size, size), f32),
            pltpu.VMEM((3, 2 * size, size), f32),
            pltpu.VMEM((3, half, size), f32),
            pltpu.VMEM((3, half, size), f32),
            pltpu.VMEM((modes, rows, 2, 3, part, size), f32),
            pltpu.VMEM((rows, 2, 3, part, size), f32),
            pltpu.VMEM((rows, 2, 3, part, size), f32),
            pltpu.VMEM((2, rows, 3, part, size), f32),
            pltpu.VMEM((3, part, size), f32),
            pltpu.VMEM((deep // 2, 3, part, size), f32),
            pltpu.VMEM((2, part, size), f32),
            pltpu.SMEM(pos.shape, jnp.int32),
            pltpu.SemaphoreType.REGULAR((2, 4)),
            dma((13,)),
            dma((8,)),
            dma((rows,)),
            dma((rows,)),
            dma((2 * rows,)),
            dma((2 * rows,)),
            dma((deep // 2,)),
            dma((deep // 2,)),
            dma((4 * rows,)),
            dma((4 * rows,)),
            dma((2,)),
            dma((2,)),
            dma((2,)),
            dma((2,)),
        ],
        compiler_params=pltpu.CompilerParams(
            collective_id=0, has_side_effects=True, vmem_limit_bytes=20 * 2**20
        ),
        name="object_pass",
    )(in_hbm(pos), cnt, in_hbm(obj), in_hbm(probe), in_hbm(amp), in_hbm(tables))
    return pl.pallas_call(
        finish_kernel,
        out_shape=(
            jax.ShapeDtypeStruct((2, size, size), f32),
            jax.ShapeDtypeStruct(probe.shape, f32),
        ),
        in_specs=[VMEM, VMEM],
        out_specs=(HBM, HBM),
        scratch_shapes=[pltpu.VMEM(probe.shape, f32), pltpu.SemaphoreType.DMA((1 + modes,))],
        compiler_params=pltpu.CompilerParams(vmem_limit_bytes=4 * 2**20),
        name="finish",
    )(new_obj, gathered)


def on_device(rows, cols, object_field, probe_modes, amplitudes, positions, counts):
    return run_pass(
        positions[0, 0], counts, object_field, probe_modes, amplitudes[0, 0], rows, cols
    )


def solution(mesh):
    rows, cols = mesh.shape["row"], mesh.shape["col"]
    return jax.shard_map(
        functools.partial(on_device, rows, cols),
        mesh=mesh,
        in_specs=(
            P(None, "row", "col"),
            P(),
            P("row", "col", None, None, None),
            P("row", "col", None, None),
            P("row", "col"),
        ),
        out_specs=(P(None, "row", "col"), P()),
        check_vma=False,
    )
```
